32 devices in a mesh: grp: 2 (over x), tm: 16 (over z, y, core).
Axes of the slice: x: 2, y: 2, z: 4, core: 2. Of those that a mesh axis runs over, the one named last changes fastest.
Arguments:
- queries: bfloat16 [64, 64, 5120], P(('grp', 'tm')), parts along dimension 0, may hold values from -8 to 8
- key_states: bfloat16 [64, 64, 5120], P(('grp', 'tm')), parts along dimension 0, may hold values from -8 to 8
- value_states: bfloat16 [64, 64, 5120], P(('grp', 'tm')), parts along dimension 0, may hold values from -6 to 6
- pose_depth: bfloat16 [64, 64, 128], P(('grp', 'tm')), parts along dimension 0, may hold values from -6 to 6
- hint_weight: bfloat16 [128, 5120], replicated, may hold values from -0.5 to 0.5
- control_gain: float32 [5120], replicated, may hold values from 1 to 6
- band_offsets: int32 [64, 3], P(('grp', 'tm')), parts along dimension 0, may hold values from -2 to 2, as said below
- control_flags: int32 [64], P(('grp', 'tm')), parts along dimension 0, may hold values 0 or 1
Outputs:
- motion_out: bfloat16 [64, 64, 5120], P(('grp', 'tm')), parts along dimension 0
The draws below stay inside these ranges and needn't reach their ends.
There are 2 independent parts, one for each index of `grp`. The reference program is written for one: setup_inputs(seed, part) draws one part's arguments, and reference() takes and returns one part's arrays. A program takes and returns all parts, laid end to end along the dimension named above; an argument that names none is the same for every part. Nothing has to cross between parts.
Inputs may be any that keep to these rules, and one draw needn't show every extreme that they name: `band_offsets`: each row holds 3 different offsets, the first of them 0.
All inputs are finite; a program needn't handle non-finite values. No bound on the sum of `control_flags` on one device may be relied on, other than what follows from the above.
Results may differ from the reference program's by a relative error of at most 0.012.
Values may be sent and summed in bfloat16 or wider, within the bound.
No kernel may reach another device: no remote copies, remote signals or barrier semaphores. Data moves between devices by JAX's collectives and lax.ppermute only.
A program may use at most 64 MiB of HBM per device.

```python
import math
import jax
import jax.numpy as jnp
from jax import lax

D = 5120
HEADS = 40
HEAD_DIM = 128
PD = 128
BAND = 2
SPANS = 3
TOK_FRAME = 64
FRAMES = 32


def paired_states(key):
    full_shape = (FRAMES, TOK_FRAME, D)
    query_draw = jax.random.normal(jax.random.fold_in(key, 101), full_shape, jnp.float32)
    key_draw = jax.random.normal(jax.random.fold_in(key, 102), full_shape, jnp.float32)
    return (jnp.clip(query_draw, -8.0, 8.0), jnp.clip(key_draw, -8.0, 8.0))


def draw_queries(key, part):
    return paired_states(key)[0].astype(jnp.bfloat16)


def draw_key_states(key, part):
    return paired_states(key)[1].astype(jnp.bfloat16)


def draw_band_offsets(key, part):
    drawn = jax.random.randint(jax.random.fold_in(key, 201), (FRAMES, 2 * BAND), 0, 1 << 20)
    ranked = drawn * (2 * BAND) + jnp.arange(2 * BAND, dtype=jnp.int32)[None, :]
    order = jnp.argsort(ranked, axis=1)
    picked = order[:, :SPANS - 1]
    table = jnp.concatenate([jnp.arange(-BAND, 0, dtype=jnp.int32), jnp.arange(1, BAND + 1, dtype=jnp.int32)])
    others = jnp.take(table, picked)
    return jnp.concatenate([jnp.zeros((FRAMES, 1), jnp.int32), others], axis=1).astype(jnp.int32)


def with_ends(result, rng, low, largest):
    longest = result.shape.index(max(result.shape))
    spots = []
    for shift in (0, 1):
        where = [jax.random.randint(jax.random.fold_in(rng, axis), (), 0, length) for axis, length in enumerate(result.shape)]
        where[longest] = (where[longest] + shift) % result.shape[longest]
        spots.append(tuple(where))
    return result.at[spots[0]].set(low).at[spots[1]].set(largest)


def level_of(key, shape, split, least, largest):
    factor_of = 1.0
    for axis_at, shards_of in split:
        heights = jax.random.uniform(jax.random.fold_in(jax.random.fold_in(key, 6), axis_at), (shards_of,), jnp.float32, least / len(split), largest / len(split))
        factor_of = factor_of * jnp.repeat(jnp.exp(heights), shape[axis_at] // shards_of).reshape((-1,) + (1,) * (len(shape) - 1 - axis_at))
    return factor_of


def noise(key, dims, width, limit, split=(), held_as=jnp.bfloat16):
    array = jax.random.normal(key, dims, jnp.float32) * width
    if len(split) > 0:
        array = level_of(key, dims, split, -0.22, 0.18) * array
    return jnp.clip(array, min=-limit, max=limit).astype(held_as)


def setup_inputs(seed: int = 0, part: int = 0) -> dict:
    seeds = jax.random.split(jax.random.key(seed), 9)
    own_keys = jax.random.split(jax.random.fold_in(seeds[8], part), 9)
    queries = draw_queries(jax.random.fold_in(jax.random.fold_in(seeds[8], part), 71), part)
    key_states = draw_key_states(jax.random.fold_in(jax.random.fold_in(seeds[8], part), 71), part)
    value_states = noise(own_keys[2], (FRAMES, TOK_FRAME, D), 1.0, 6.0, ((0, 16),))
    pose_depth = noise(own_keys[3], (FRAMES, TOK_FRAME, PD), 1.0, 6.0, ((0, 16),))
    hint_weight = noise(seeds[4], (PD, D), PD ** -0.5, 0.5)
    control_gain = jnp.clip(jnp.exp(jax.random.uniform(seeds[5], (D,), jnp.float32, math.log(1.0), math.log(6.0))), 1.0, 6.0)
    band_offsets = draw_band_offsets(jax.random.fold_in(jax.random.fold_in(seeds[8], part), 71), part)
    control_flags = with_ends((jax.random.randint(own_keys[7], (FRAMES,), 0, 4) < 3).astype(jnp.int32), jax.random.fold_in(own_keys[7], 1), 0, 1)
    return dict(queries=queries, key_states=key_states, value_states=value_states, pose_depth=pose_depth, hint_weight=hint_weight, control_gain=control_gain, band_offsets=band_offsets, control_flags=control_flags)


def round_sum(first, second):
    return (first.astype(jnp.float32) + second.astype(jnp.float32)).astype(jnp.bfloat16)


def attend(query_set, key_set, value_set, band_offsets):
    frame_total = query_set.shape[0]
    score_scale = HEAD_DIM ** -0.5

    def single(position):
        chosen = ((position + band_offsets[position]) % frame_total).astype(jnp.int32)
        query_rows = query_set[position].astype(jnp.float32).reshape(TOK_FRAME, HEADS, HEAD_DIM)
        key_rows = jnp.take(key_set, chosen, axis=0).astype(jnp.float32).reshape(SPANS * TOK_FRAME, HEADS, HEAD_DIM)
        value_rows = jnp.take(value_set, chosen, axis=0).astype(jnp.float32).reshape(SPANS * TOK_FRAME, HEADS, HEAD_DIM)
        scores = jnp.einsum("qhd,khd->hqk", query_rows, key_rows) * score_scale
        weights = lax.optimization_barrier(jax.nn.softmax(scores, axis=-1).astype(jnp.bfloat16))
        attended = jnp.einsum("hqk,khd->qhd", weights.astype(jnp.float32), value_rows)
        return attended.reshape(TOK_FRAME, D).astype(jnp.bfloat16)

    return lax.map(single, jnp.arange(frame_total, dtype=jnp.int32))


def reference(queries, key_states, value_states, pose_depth, hint_weight, control_gain, band_offsets, control_flags):
    projected = jnp.dot(pose_depth.reshape(-1, PD), hint_weight, preferred_element_type=jnp.float32)
    hint_rows = projected.astype(jnp.bfloat16).reshape(FRAMES, TOK_FRAME, D)
    control_queries = round_sum(queries, hint_rows)
    control_keys = round_sum(key_states, hint_rows)
    control_values = round_sum(value_states, hint_rows)
    control_out = attend(control_queries, control_keys, control_values, band_offsets)
    gate_scale = control_flags.astype(jnp.float32)[:, None, None] * control_gain.astype(jnp.float32)[None, None, :]
    residual = (gate_scale * control_out.astype(jnp.float32)).astype(jnp.bfloat16)
    mixed_values = round_sum(value_states, residual)
    return attend(queries, key_states, mixed_values, band_offsets)
```

```python
import jax
import jax.numpy as jnp
from jax import lax
from jax.experimental import pallas as pl
from jax.experimental.pallas import tpu as pltpu
from jax.sharding import PartitionSpec as P

HEAD_DIM = 128
BAND = 2
GROUP = 4
SLICES = (3, 4, 3)
META = 8
F32 = jnp.float32
BF16 = jnp.bfloat16
I32 = jnp.int32
ANY = pl.BlockSpec(memory_space=pl.ANY)
SMEM = pl.BlockSpec(memory_space=pltpu.SMEM)


def run(kernel, ins, outs, scratch, copies, scalars=(), aliases=None, work=(1, 1)):
    a, b, c, d = len(scalars), len(ins), len(outs), len(scratch)

    def body(*refs):
        kernel(refs[:a], refs[a : a + b], refs[a + b : a + b + c], refs[a + b + c : a + b + c + d], refs[-1])

    return pl.pallas_call(
        body,
        out_shape=list(outs),
        in_specs=[SMEM] * a + [ANY] * b,
        out_specs=[ANY] * c,
        scratch_shapes=[*scratch, pltpu.SemaphoreType.DMA((copies,))],
        input_output_aliases=aliases or {},
        compiler_params=pltpu.CompilerParams(vmem_limit_bytes=24 * 1024 * 1024),
        cost_estimate=pl.CostEstimate(flops=work[0], bytes_accessed=work[1], transcendentals=0),
    )(*scalars, *ins)


def move(pairs, sems):
    copies = [pltpu.make_async_copy(s, d, sems.at[i]) for i, (s, d) in enumerate(pairs)]
    for copy in copies:
        copy.start()
    for copy in copies:
        copy.wait()


def lanes(me, quarter, first, width):
    return pl.ds(pl.multiple_of(me * quarter + first, HEAD_DIM), width)


def rows(shape, dtype=BF16):
    return jax.ShapeDtypeStruct(shape, dtype)


def pack_pair(me, keys, values, lead, quarter, first, width):
    frames, toks, _ = keys.shape

    def kernel(scalars, ins, outs, scratch, sems):
        mine = scalars[0][0]
        pairs = []
        if lead:
            offsets, flags = scalars[1:]
            spans = offsets.shape[1]
            row = lax.broadcasted_iota(I32, (toks, HEAD_DIM), 0)
            col = lax.broadcasted_iota(I32, (toks, HEAD_DIM), 1)
            block = jnp.zeros((toks, HEAD_DIM), F32)
            for f in range(frames):
                for j in range(spans):
                    block = jnp.where((row == f) & (col == j), offsets[f, j].astype(F32), block)
                block = jnp.where((row == f) & (col == spans), flags[f].astype(F32), block)
            scratch[0][...] = block.astype(BF16)
        for k in range(GROUP):
            where = lanes(mine ^ k, quarter, first, width)
            pairs.append((ins[0].at[:, :, where], outs[k].at[pl.ds(0, frames)]))
            pairs.append((ins[1].at[:, :, where], outs[k].at[pl.ds(frames, frames)]))
            if lead:
                for f in range(frames):
                    pairs.append((ins[2].at[f], outs[k].at[2 * frames, :, pl.ds(f * HEAD_DIM, HEAD_DIM)]))
                pairs.append((scratch[0], outs[k].at[2 * frames, :, pl.ds(frames * HEAD_DIM, HEAD_DIM)]))
        move(pairs, sems)

    shape = (2 * frames + (1 if lead else 0), toks, width)
    return run(
        kernel,
        [keys, values, *lead[:1]],
        [rows(shape)] * GROUP,
        [pltpu.VMEM((toks, HEAD_DIM), BF16)] if lead else [],
        GROUP * (2 + (frames + 1 if lead else 0)),
        [me, *lead[1:]],
        work=(1, 16 * frames * toks * width),
    )


def pack_one(me, array, quarter, first, width):
    frames, toks, _ = array.shape

    def kernel(scalars, ins, outs, scratch, sems):
        mine = scalars[0][0]
        move([(ins[0].at[:, :, lanes(mine ^ k, quarter, first, width)], outs[k]) for k in range(GROUP)], sems)

    return run(
        kernel, [array], [rows((frames, toks, width))] * GROUP, [], GROUP, [me], work=(1, 16 * frames * toks * width)
    )


def edges(me, parts):
    def kernel(scalars, ins, outs, scratch, sems):
        mine = scalars[0][0]
        for i, owner in enumerate((GROUP - 1, 0)):
            for k in range(GROUP):

                @pl.when((mine ^ k) == owner)
                def _(i=i, k=k):
                    pltpu.make_async_copy(ins[k], outs[i], sems.at[i]).start()

        for i in range(2):
            pltpu.make_async_copy(ins[0], outs[i], sems.at[i]).wait()

    shape = rows(parts[0].shape)
    return run(kernel, parts, [shape, shape], [], 2, [me], work=(1, 8 * parts[0].size))


def attend(query, keys, values):
    scores = lax.dot_general(query, keys, (((1,), (1,)), ((), ())), preferred_element_type=F32) * HEAD_DIM ** (-0.5)
    scores = jnp.exp(scores - jnp.max(scores, axis=1, keepdims=True))
    weights = (scores * (1.0 / jnp.sum(scores, axis=1, keepdims=True))).astype(BF16)
    return jnp.dot(weights, values, preferred_element_type=F32).astype(BF16)


def band(ref, spots, cols):
    return jnp.concatenate([ref[s, :, cols] for s in spots], axis=0)


def hint_branch(me, pairs_in, queries, before, after, weight, gain, setting, spans, quarter, first, width):
    frames, toks, _ = queries[0].shape
    lead = setting is None
    total, wide = GROUP * frames, GROUP * frames + 2 * BAND

    def kernel(scalars, ins, outs, scratch, sems):
        mine = scalars[0][0]
        kv, qs, (prev, after_ref, w_hbm, g_hbm) = ins[:GROUP], ins[GROUP : 2 * GROUP], ins[2 * GROUP : 2 * GROUP + 4]
        q_s, k_s, v_s, c_s, m_s, p_s, w_s, g_s = scratch[:8]
        where = lanes(mine, quarter, first, width)
        todo = [(w_hbm.at[:, where], w_s), (g_hbm.at[:, where], g_s)]
        for k in range(GROUP):
            todo.append((qs[k], q_s.at[pl.ds((mine ^ k) * frames, frames)]))
        for k, src in enumerate([*kv, prev, after_ref]):
            at = BAND + (mine ^ k) * frames if k < GROUP else (0 if k == GROUP else BAND + total)
            todo.append((src.at[pl.ds(0, frames)], k_s.at[pl.ds(at, frames)]))
            todo.append((src.at[pl.ds(frames, frames)], v_s.at[pl.ds(at, frames)]))
            if lead:
                for f in range(frames):
                    todo.append((src.at[2 * frames, :, pl.ds(f * HEAD_DIM, HEAD_DIM)], p_s.at[at + f]))
                if k < GROUP:
                    block = src.at[2 * frames, pl.ds(0, 2 * META), pl.ds(frames * HEAD_DIM, HEAD_DIM)]
                    todo.append((block, scratch[8].at[mine ^ k]))
        if not lead:
            todo.append((ins[-1], p_s))
        move(todo, sems)
        if lead:
            meta_bf, meta_v, meta = scratch[8:]
            for s in range(GROUP):
                meta_v[s] = meta_bf[s].astype(F32).astype(I32)[:META]
            move([(meta_v, meta), (meta_v, outs[4]), (p_s, outs[3])], sems)
        else:
            meta = scalars[1]

        def hints(f, _):
            hint = jnp.dot(p_s[f], w_s[...], preferred_element_type=F32).astype(BF16).astype(F32)
            k_s[f] = (k_s[f].astype(F32) + hint).astype(BF16)
            c_s[f] = (v_s[f].astype(F32) + hint).astype(BF16)
            at = f - BAND

            @pl.when((at >= 0) & (at < total))
            def _():
                q_s[at] = (q_s[at].astype(F32) + hint).astype(BF16)

            return 0

        lax.fori_loop(0, wide, hints, 0)

        def frame(f, _):
            s, r = lax.div(f, frames), lax.rem(f, frames)
            spots = [BAND + f + meta[s, r, j] for j in range(spans)]
            flag = meta[s, r, spans].astype(F32)
            for h in range(width // HEAD_DIM):
                cols = slice(h * HEAD_DIM, (h + 1) * HEAD_DIM)
                out = attend(q_s[f, :, cols], band(k_s, spots, cols), band(c_s, spots, cols))
                residual = (flag * g_s[:, cols] * out.astype(F32)).astype(BF16)
                m_s[f, :, cols] = (v_s[BAND + f, :, cols].astype(F32) + residual.astype(F32)).astype(BF16)
            return 0

        lax.fori_loop(0, total, frame, 0)
        move([(m_s, outs[0]), (m_s.at[pl.ds(total - BAND, BAND)], outs[1]), (m_s.at[pl.ds(0, BAND)], outs[2])], sems)

    outs = [rows((total, toks, width)), rows((BAND, toks, width)), rows((BAND, toks, width))]
    scratch = [
        pltpu.VMEM((total, toks, width), BF16),
        pltpu.VMEM((wide, toks, width), BF16),
        pltpu.VMEM((wide, toks, width), BF16),
        pltpu.VMEM((wide, toks, width), BF16),
        pltpu.VMEM((total, toks, width), BF16),
        pltpu.VMEM((wide, toks, HEAD_DIM), BF16),
        pltpu.VMEM((HEAD_DIM, width), BF16),
        pltpu.VMEM((1, width), F32),
    ]
    ins = [*pairs_in, *queries, before, after, weight, gain]
    scalars = [me]
    if lead:
        outs += [rows((wide, toks, HEAD_DIM)), rows((GROUP, META, HEAD_DIM), I32)]
        scratch += [
            pltpu.VMEM((GROUP, 2 * META, HEAD_DIM), BF16),
            pltpu.VMEM((GROUP, META, HEAD_DIM), I32),
            pltpu.SMEM((GROUP, META, HEAD_DIM), I32),
        ]
    else:
        ins.append(setting[0])
        scalars.append(setting[1])
    work = (4 * total * toks * spans * toks * width, 10 * total * toks * width)
    return run(kernel, ins, outs, scratch, 3 + GROUP + (GROUP + 2) * (3 + frames), scalars, work=work)


def base_block(me, pairs_in, queries, before, after, mixed, mixed_before, mixed_after, meta, spans):
    frames, toks, width = queries[0].shape
    total, wide = GROUP * frames, GROUP * frames + 2 * BAND

    def kernel(scalars, ins, outs, scratch, sems):
        mine, meta = scalars[0][0], scalars[1]
        kv, qs, (prev, after_ref) = ins[:GROUP], ins[GROUP : 2 * GROUP], ins[2 * GROUP : 2 * GROUP + 2]
        q_s, k_s, m_s, o_s = scratch
        todo = [
            (ins[-3], m_s.at[pl.ds(BAND, total)]),
            (ins[-2], m_s.at[pl.ds(0, BAND)]),
            (ins[-1], m_s.at[pl.ds(BAND + total, BAND)]),
            (prev.at[pl.ds(0, frames)], k_s.at[pl.ds(0, BAND)]),
            (after_ref.at[pl.ds(0, frames)], k_s.at[pl.ds(BAND + total, BAND)]),
        ]
        for k in range(GROUP):
            at = (mine ^ k) * frames
            todo.append((qs[k], q_s.at[pl.ds(at, frames)]))
            todo.append((kv[k].at[pl.ds(0, frames)], k_s.at[pl.ds(BAND + at, frames)]))
        move(todo, sems)

        def frame(f, _):
            s, r = lax.div(f, frames), lax.rem(f, frames)
            spots = [BAND + f + meta[s, r, j] for j in range(spans)]
            for h in range(width // HEAD_DIM):
                cols = slice(h * HEAD_DIM, (h + 1) * HEAD_DIM)
                o_s[f, :, cols] = attend(q_s[f, :, cols], band(k_s, spots, cols), band(m_s, spots, cols))
            return 0

        lax.fori_loop(0, total, frame, 0)
        move([(o_s.at[pl.ds((mine ^ k) * frames, frames)], outs[k]) for k in range(GROUP)], sems)

    scratch = [
        pltpu.VMEM((total, toks, width), BF16),
        pltpu.VMEM((wide, toks, width), BF16),
        pltpu.VMEM((wide, toks, width), BF16),
        pltpu.VMEM((total, toks, width), BF16),
    ]
    ins = [*pairs_in, *queries, before, after, mixed, mixed_before, mixed_after]
    work = (4 * total * toks * spans * toks * width, 8 * total * toks * width)
    return run(kernel, ins, [rows((frames, toks, width))] * GROUP, scratch, 5 + 2 * GROUP, [me, meta], work=work)


def place(me, parts, into, model_width, quarter, first):
    frames, toks, width = parts[0].shape

    def kernel(scalars, ins, outs, scratch, sems):
        mine = scalars[0][0]
        move([(ins[k], outs[0].at[:, :, lanes(mine ^ k, quarter, first, width)]) for k in range(GROUP)], sems)

    held = [] if into is None else [into]
    return run(
        kernel,
        [*parts, *held],
        [rows((frames, toks, model_width))],
        [],
        GROUP,
        [me],
        {} if into is None else {1 + GROUP: 0},
        (1, 16 * frames * toks * width),
    )[0]


def solution(mesh):
    count = mesh.shape["tm"]
    assert count % GROUP == 0
    across = [[(i, i ^ k) for i in range(count)] for k in range(GROUP)]
    upward = [(i, (i + GROUP) % count) for i in range(count)]
    downward = [(i, (i - GROUP) % count) for i in range(count)]

    def exchange(parts):
        return [parts[0]] + [lax.ppermute(parts[k], "tm", across[k]) for k in range(1, GROUP)]

    def body(queries, key_states, value_states, pose_depth, hint_weight, control_gain, band_offsets, control_flags):
        frames, _, model_width = queries.shape
        spans = band_offsets.shape[1]
        quarter = model_width // GROUP
        assert frames == BAND and sum(SLICES) * HEAD_DIM == quarter
        me = lax.rem(lax.axis_index("tm"), GROUP).astype(I32).reshape(1)
        gain = control_gain.reshape(1, -1)
        cuts = [(sum(SLICES[:c]) * HEAD_DIM, n * HEAD_DIM) for c, n in enumerate(SLICES)]
        state = []
        for c, (first, width) in enumerate(cuts):
            lead = [pose_depth, band_offsets, control_flags] if c == 0 else []
            pair = exchange(pack_pair(me, key_states, value_states, lead, quarter, first, width))
            state.append(pair)
        sides, asked = [], []
        for c, (first, width) in enumerate(cuts):
            last, start = edges(me, state[c])
            sides.append((lax.ppermute(last, "tm", upward), lax.ppermute(start, "tm", downward)))
            asked.append(exchange(pack_one(me, queries, quarter, first, width)))
        setting, mixed = None, []
        for c, (first, width) in enumerate(cuts):
            got = hint_branch(
                me, state[c], asked[c], *sides[c], hint_weight, gain, setting, spans, quarter, first, width
            )
            if setting is None:
                setting = got[3:]
            mixed.append((got[0], lax.ppermute(got[1], "tm", upward), lax.ppermute(got[2], "tm", downward)))
        out = None
        for c, (first, width) in enumerate(cuts):
            parts = base_block(me, state[c], asked[c], *sides[c], *mixed[c], setting[1], spans)
            out = place(me, exchange(parts), out, model_width, quarter, first)
        return out

    return jax.shard_map(
        body,
        mesh=mesh,
        in_specs=(
            P(("grp", "tm"), None, None),
            P(("grp", "tm"), None, None),
            P(("grp", "tm"), None, None),
            P(("grp", "tm"), None, None),
            P(),
            P(),
            P(("grp", "tm"), None),
            P(("grp", "tm")),
        ),
        out_specs=P(("grp", "tm"), None, None),
        check_vma=False,
    )
```

```python
import jax
import jax.numpy as jnp
from jax import lax
from jax.experimental import pallas as pl
from jax.experimental.pallas import tpu as pltpu
from jax.sharding import PartitionSpec as P

HEAD_DIM = 128
BAND = 2
GROUP = 4
SLICES = (3, 4, 3)
META = 8
F32 = jnp.float32
BF16 = jnp.bfloat16
I32 = jnp.int32
ANY = pl.BlockSpec(memory_space=pl.ANY)
SMEM = pl.BlockSpec(memory_space=pltpu.SMEM)


def run(kernel, ins, outs, scratch, copies, scalars=(), aliases=None, work=(1, 1)):
    a, b, c, d = len(scalars), len(ins), len(outs), len(scratch)

    def body(*refs):
        kernel(refs[:a], refs[a : a + b], refs[a + b : a + b + c], refs[a + b + c : a + b + c + d], refs[-1])

    return pl.pallas_call(
        body,
        out_shape=list(outs),
        in_specs=[SMEM] * a + [ANY] * b,
        out_specs=[ANY] * c,
        scratch_shapes=[*scratch, pltpu.SemaphoreType.DMA((copies,))],
        input_output_aliases=aliases or {},
        compiler_params=pltpu.CompilerParams(vmem_limit_bytes=24 * 1024 * 1024),
        cost_estimate=pl.CostEstimate(flops=work[0], bytes_accessed=work[1], transcendentals=0),
    )(*scalars, *ins)


def move(pairs, sems):
    copies = [pltpu.make_async_copy(s, d, sems.at[i]) for i, (s, d) in enumerate(pairs)]
    for copy in copies:
        copy.start()
    for copy in copies:
        copy.wait()


def lanes(me, quarter, first, width):
    return pl.ds(pl.multiple_of(me * quarter + first, HEAD_DIM), width)


def rows(shape, dtype=BF16):
    return jax.ShapeDtypeStruct(shape, dtype)


def pack_pair(me, keys, values, lead, quarter, first, width):
    frames, toks, _ = keys.shape

    def kernel(scalars, ins, outs, scratch, sems):
        mine = scalars[0][0]
        pairs = []
        if lead:
            offsets, flags = scalars[1:]
            spans = offsets.shape[1]
            row = lax.broadcasted_iota(I32, (toks, HEAD_DIM), 0)
            col = lax.broadcasted_iota(I32, (toks, HEAD_DIM), 1)
            block = jnp.zeros((toks, HEAD_DIM), F32)
            for f in range(frames):
                for j in range(spans):
                    block = jnp.where((row == f) & (col == j), offsets[f, j].astype(F32), block)
                block = jnp.where((row == f) & (col == spans), flags[f].astype(F32), block)
            scratch[0][...] = block.astype(BF16)
        for k in range(GROUP):
            where = lanes(mine ^ k, quarter, first, width)
            pairs.append((ins[0].at[:, :, where], outs[k].at[pl.ds(0, frames)]))
            pairs.append((ins[1].at[:, :, where], outs[k].at[pl.ds(frames, frames)]))
            if lead:
                for f in range(frames):
                    pairs.append((ins[2].at[f], outs[k].at[2 * frames, :, pl.ds(f * HEAD_DIM, HEAD_DIM)]))
                pairs.append((scratch[0], outs[k].at[2 * frames, :, pl.ds(frames * HEAD_DIM, HEAD_DIM)]))
        move(pairs, sems)

    shape = (2 * frames + (1 if lead else 0), toks, width)
    return run(
        kernel,
        [keys, values, *lead[:1]],
        [rows(shape)] * GROUP,
        [pltpu.VMEM((toks, HEAD_DIM), BF16)] if lead else [],
        GROUP * (2 + (frames + 1 if lead else 0)),
        [me, *lead[1:]],
        work=(1, 16 * frames * toks * width),
    )


def pack_one(me, array, quarter, first, width):
    frames, toks, _ = array.shape

    def kernel(scalars, ins, outs, scratch, sems):
        mine = scalars[0][0]
        move([(ins[0].at[:, :, lanes(mine ^ k, quarter, first, width)], outs[k]) for k in range(GROUP)], sems)

    return run(
        kernel, [array], [rows((frames, toks, width))] * GROUP, [], GROUP, [me], work=(1, 16 * frames * toks * width)
    )


def edges(me, parts):
    def kernel(scalars, ins, outs, scratch, sems):
        mine = scalars[0][0]
        for i, owner in enumerate((GROUP - 1, 0)):
            for k in range(GROUP):

                @pl.when((mine ^ k) == owner)
                def _(i=i, k=k):
                    pltpu.make_async_copy(ins[k], outs[i], sems.at[i]).start()

        for i in range(2):
            pltpu.make_async_copy(ins[0], outs[i], sems.at[i]).wait()

    shape = rows(parts[0].shape)
    return run(kernel, parts, [shape, shape], [], 2, [me], work=(1, 8 * parts[0].size))


def attend(jobs):
    scores = [
        lax.dot_general(query, keys, (((1,), (1,)), ((), ())), preferred_element_type=F32) * HEAD_DIM ** (-0.5)
        for query, keys, _ in jobs
    ]
    tops = [jnp.max(x, axis=1, keepdims=True) for x in scores]
    scores = [jnp.exp(x - top) for x, top in zip(scores, tops)]
    scales = [1.0 / jnp.sum(x, axis=1, keepdims=True) for x in scores]
    weights = [(x * scale).astype(BF16) for x, scale in zip(scores, scales)]
    return [
        jnp.dot(w, values, preferred_element_type=F32).astype(BF16) for w, (_, _, values) in zip(weights, jobs)
    ]


def band(ref, spots, cols):
    return jnp.concatenate([ref[s, :, cols] for s in spots], axis=0)


def hint_branch(me, pairs_in, queries, before, after, weight, gain, setting, spans, quarter, first, width):
    frames, toks, _ = queries[0].shape
    lead = setting is None
    total, wide = GROUP * frames, GROUP * frames + 2 * BAND

    def kernel(scalars, ins, outs, scratch, sems):
        mine = scalars[0][0]
        kv, qs, (prev, after_ref, w_hbm, g_hbm) = ins[:GROUP], ins[GROUP : 2 * GROUP], ins[2 * GROUP : 2 * GROUP + 4]
        q_s, k_s, v_s, c_s, m_s, p_s, w_s, g_s = scratch[:8]
        where = lanes(mine, quarter, first, width)
        todo = [(w_hbm.at[:, where], w_s), (g_hbm.at[:, where], g_s)]
        for k in range(GROUP):
            todo.append((qs[k], q_s.at[pl.ds((mine ^ k) * frames, frames)]))
        for k, src in enumerate([*kv, prev, after_ref]):
            at = BAND + (mine ^ k) * frames if k < GROUP else (0 if k == GROUP else BAND + total)
            todo.append((src.at[pl.ds(0, frames)], k_s.at[pl.ds(at, frames)]))
            todo.append((src.at[pl.ds(frames, frames)], v_s.at[pl.ds(at, frames)]))
            if lead:
                for f in range(frames):
                    todo.append((src.at[2 * frames, :, pl.ds(f * HEAD_DIM, HEAD_DIM)], p_s.at[at + f]))
                if k < GROUP:
                    block = src.at[2 * frames, pl.ds(0, 2 * META), pl.ds(frames * HEAD_DIM, HEAD_DIM)]
                    todo.append((block, scratch[8].at[mine ^ k]))
        if not lead:
            todo.append((ins[-1], p_s))
        move(todo, sems)
        if lead:
            meta_bf, meta_v, meta = scratch[8:]
            for s in range(GROUP):
                meta_v[s] = meta_bf[s].astype(F32).astype(I32)[:META]
            move([(meta_v, meta), (meta_v, outs[4]), (p_s, outs[3])], sems)
        else:
            meta = scalars[1]

        def hints(f, _):
            hint = jnp.dot(p_s[f], w_s[...], preferred_element_type=F32).astype(BF16).astype(F32)
            k_s[f] = (k_s[f].astype(F32) + hint).astype(BF16)
            c_s[f] = (v_s[f].astype(F32) + hint).astype(BF16)
            at = f - BAND

            @pl.when((at >= 0) & (at < total))
            def _():
                q_s[at] = (q_s[at].astype(F32) + hint).astype(BF16)

            return 0

        lax.fori_loop(0, wide, hints, 0)

        heads = [slice(h * HEAD_DIM, (h + 1) * HEAD_DIM) for h in range(width // HEAD_DIM)]

        def joint(s, _):
            at, jobs = [], []
            for r in range(frames):
                f = s * frames + r
                spots = [BAND + f + meta[s, r, j] for j in range(spans)]
                for cols in heads:
                    at.append((f, meta[s, r, spans].astype(F32), cols))
                    jobs.append((q_s[f, :, cols], band(k_s, spots, cols), band(c_s, spots, cols)))
            for (f, flag, cols), out in zip(at, attend(jobs)):
                residual = (flag * g_s[:, cols] * out.astype(F32)).astype(BF16)
                m_s[f, :, cols] = (v_s[BAND + f, :, cols].astype(F32) + residual.astype(F32)).astype(BF16)
            return 0

        lax.fori_loop(0, GROUP, joint, 0)
        move([(m_s, outs[0]), (m_s.at[pl.ds(total - BAND, BAND)], outs[1]), (m_s.at[pl.ds(0, BAND)], outs[2])], sems)

    outs = [rows((total, toks, width)), rows((BAND, toks, width)), rows((BAND, toks, width))]
    scratch = [
        pltpu.VMEM((total, toks, width), BF16),
        pltpu.VMEM((wide, toks, width), BF16),
        pltpu.VMEM((wide, toks, width), BF16),
        pltpu.VMEM((wide, toks, width), BF16),
        pltpu.VMEM((total, toks, width), BF16),
        pltpu.VMEM((wide, toks, HEAD_DIM), BF16),
        pltpu.VMEM((HEAD_DIM, width), BF16),
        pltpu.VMEM((1, width), F32),
    ]
    ins = [*pairs_in, *queries, before, after, weight, gain]
    scalars = [me]
    if lead:
        outs += [rows((wide, toks, HEAD_DIM)), rows((GROUP, META, HEAD_DIM), I32)]
        scratch += [
            pltpu.VMEM((GROUP, 2 * META, HEAD_DIM), BF16),
            pltpu.VMEM((GROUP, META, HEAD_DIM), I32),
            pltpu.SMEM((GROUP, META, HEAD_DIM), I32),
        ]
    else:
        ins.append(setting[0])
        scalars.append(setting[1])
    work = (4 * total * toks * spans * toks * width, 10 * total * toks * width)
    return run(kernel, ins, outs, scratch, 3 + GROUP + (GROUP + 2) * (3 + frames), scalars, work=work)


def base_block(me, pairs_in, queries, before, after, mixed, mixed_before, mixed_after, meta, spans):
    frames, toks, width = queries[0].shape
    total, wide = GROUP * frames, GROUP * frames + 2 * BAND

    def kernel(scalars, ins, outs, scratch, sems):
        mine, meta = scalars[0][0], scalars[1]
        kv, qs, (prev, after_ref) = ins[:GROUP], ins[GROUP : 2 * GROUP], ins[2 * GROUP : 2 * GROUP + 2]
        q_s, k_s, m_s, o_s = scratch
        todo = [
            (ins[-3], m_s.at[pl.ds(BAND, total)]),
            (ins[-2], m_s.at[pl.ds(0, BAND)]),
            (ins[-1], m_s.at[pl.ds(BAND + total, BAND)]),
            (prev.at[pl.ds(0, frames)], k_s.at[pl.ds(0, BAND)]),
            (after_ref.at[pl.ds(0, frames)], k_s.at[pl.ds(BAND + total, BAND)]),
        ]
        for k in range(GROUP):
            at = (mine ^ k) * frames
            todo.append((qs[k], q_s.at[pl.ds(at, frames)]))
            todo.append((kv[k].at[pl.ds(0, frames)], k_s.at[pl.ds(BAND + at, frames)]))
        move(todo, sems)

        heads = [slice(h * HEAD_DIM, (h + 1) * HEAD_DIM) for h in range(width // HEAD_DIM)]

        def joint(s, _):
            at, jobs = [], []
            for r in range(frames):
                f = s * frames + r
                spots = [BAND + f + meta[s, r, j] for j in range(spans)]
                for cols in heads:
                    at.append((f, cols))
                    jobs.append((q_s[f, :, cols], band(k_s, spots, cols), band(m_s, spots, cols)))
            for (f, cols), out in zip(at, attend(jobs)):
                o_s[f, :, cols] = out
            return 0

        lax.fori_loop(0, GROUP, joint, 0)
        move([(o_s.at[pl.ds((mine ^ k) * frames, frames)], outs[k]) for k in range(GROUP)], sems)

    scratch = [
        pltpu.VMEM((total, toks, width), BF16),
        pltpu.VMEM((wide, toks, width), BF16),
        pltpu.VMEM((wide, toks, width), BF16),
        pltpu.VMEM((total, toks, width), BF16),
    ]
    ins = [*pairs_in, *queries, before, after, mixed, mixed_before, mixed_after]
    work = (4 * total * toks * spans * toks * width, 8 * total * toks * width)
    return run(kernel, ins, [rows((frames, toks, width))] * GROUP, scratch, 5 + 2 * GROUP, [me, meta], work=work)


def place(me, parts, into, model_width, quarter, first):
    frames, toks, width = parts[0].shape

    def kernel(scalars, ins, outs, scratch, sems):
        mine = scalars[0][0]
        move([(ins[k], outs[0].at[:, :, lanes(mine ^ k, quarter, first, width)]) for k in range(GROUP)], sems)

    held = [] if into is None else [into]
    return run(
        kernel,
        [*parts, *held],
        [rows((frames, toks, model_width))],
        [],
        GROUP,
        [me],
        {} if into is None else {1 + GROUP: 0},
        (1, 16 * frames * toks * width),
    )[0]


def solution(mesh):
    count = mesh.shape["tm"]
    assert count % GROUP == 0
    across = [[(i, i ^ k) for i in range(count)] for k in range(GROUP)]
    upward = [(i, (i + GROUP) % count) for i in range(count)]
    downward = [(i, (i - GROUP) % count) for i in range(count)]

    def exchange(parts):
        return [parts[0]] + [lax.ppermute(parts[k], "tm", across[k]) for k in range(1, GROUP)]

    def body(queries, key_states, value_states, pose_depth, hint_weight, control_gain, band_offsets, control_flags):
        frames, _, model_width = queries.shape
        spans = band_offsets.shape[1]
        quarter = model_width // GROUP
        assert frames == BAND and sum(SLICES) * HEAD_DIM == quarter
        me = lax.rem(lax.axis_index("tm"), GROUP).astype(I32).reshape(1)
        gain = control_gain.reshape(1, -1)
        cuts = [(sum(SLICES[:c]) * HEAD_DIM, n * HEAD_DIM) for c, n in enumerate(SLICES)]
        state = []
        for c, (first, width) in enumerate(cuts):
            lead = [pose_depth, band_offsets, control_flags] if c == 0 else []
            pair = exchange(pack_pair(me, key_states, value_states, lead, quarter, first, width))
            state.append(pair)
        sides, asked = [], []
        for c, (first, width) in enumerate(cuts):
            last, start = edges(me, state[c])
            sides.append((lax.ppermute(last, "tm", upward), lax.ppermute(start, "tm", downward)))
            asked.append(exchange(pack_one(me, queries, quarter, first, width)))
        setting, mixed = None, []
        for c, (first, width) in enumerate(cuts):
            got = hint_branch(
                me, state[c], asked[c], *sides[c], hint_weight, gain, setting, spans, quarter, first, width
            )
            if setting is None:
                setting = got[3:]
            mixed.append((got[0], lax.ppermute(got[1], "tm", upward), lax.ppermute(got[2], "tm", downward)))
        out = None
        for c, (first, width) in enumerate(cuts):
            parts = base_block(me, state[c], asked[c], *sides[c], *mixed[c], setting[1], spans)
            out = place(me, exchange(parts), out, model_width, quarter, first)
        return out

    return jax.shard_map(
        body,
        mesh=mesh,
        in_specs=(
            P(("grp", "tm"), None, None),
            P(("grp", "tm"), None, None),
            P(("grp", "tm"), None, None),
            P(("grp", "tm"), None, None),
            P(),
            P(),
            P(("grp", "tm"), None),
            P(("grp", "tm")),
        ),
        out_specs=P(("grp", "tm"), None, None),
        check_vma=False,
    )
```

```python
import jax
import jax.numpy as jnp
from jax import lax
from jax.experimental import pallas as pl
from jax.experimental.pallas import tpu as pltpu
from jax.sharding import PartitionSpec as P

HEAD_DIM = 128
BAND = 2
GROUP = 4
SLICES = (5, 5)
META = 8
ORDER = [("KV", 0), ("KV", 1), ("Q", 0), ("Z", 0), ("Q", 1), ("Z", 1), ("H", 0), ("H", 1), ("B", 0), ("B", 1), ("P", 0), ("P", 1)]
DEPTH_Y, DEPTH_Z = 2, 2
F32 = jnp.float32
BF16 = jnp.bfloat16
I32 = jnp.int32
VMEM = pl.BlockSpec(memory_space=pltpu.VMEM)
SMEM = pl.BlockSpec(memory_space=pltpu.SMEM)
HBM = pl.BlockSpec(memory_space=pltpu.HBM)


def run(kernel, name, ins, outs, scratch, copies, scalars=(), where=VMEM, to=VMEM, aliases=None, us=1.0):
    a, b, c, d = len(scalars), len(ins), len(outs), len(scratch)

    def body(*refs):
        kernel(refs[:a], refs[a : a + b], refs[a + b : a + b + c], refs[a + b + c : a + b + c + d], refs[-1])

    return pl.pallas_call(
        body,
        out_shape=list(outs),
        in_specs=[SMEM] * a + (where if isinstance(where, list) else [where] * b),
        out_specs=[to] * c,
        scratch_shapes=[*scratch, pltpu.SemaphoreType.DMA((max(copies, 1),))],
        input_output_aliases=aliases or {},
        compiler_params=pltpu.CompilerParams(vmem_limit_bytes=16 * 1024 * 1024),
        cost_estimate=pl.CostEstimate(flops=1, bytes_accessed=int(us * 3.4e6), transcendentals=0),
        name=name,
    )(*scalars, *ins)


def move(pairs, sems):
    copies = [pltpu.make_async_copy(s, d, sems.at[i]) for i, (s, d) in enumerate(pairs)]
    for copy in copies:
        copy.start()
    for copy in copies:
        copy.wait()


def lanes(me, quarter, first, width):
    return pl.ds(pl.multiple_of(me * quarter + first, HEAD_DIM), width)


def rows(shape, dtype=BF16):
    return jax.ShapeDtypeStruct(shape, dtype)


def pack_pair(me, keys, values, lead, quarter, first, width):
    frames, toks, _ = keys.shape

    def kernel(scalars, ins, outs, scratch, sems):
        mine = scalars[0][0]
        pairs = []
        for k in (1, 2, 3, 0):
            where = lanes(mine ^ k, quarter, first, width)
            pairs.append((ins[0].at[:, :, where], outs[k].at[pl.ds(0, frames)]))
            pairs.append((ins[1].at[:, :, where], outs[k].at[pl.ds(frames, frames)]))
            if lead:
                for f in range(frames):
                    pairs.append((ins[2].at[f], outs[k].at[2 * frames, :, pl.ds(f * HEAD_DIM, HEAD_DIM)]))
        if lead:
            offsets, flags = scalars[1:]
            spans = offsets.shape[1]
            row = lax.broadcasted_iota(I32, (toks, HEAD_DIM), 0)
            col = lax.broadcasted_iota(I32, (toks, HEAD_DIM), 1)
            block = jnp.zeros((toks, HEAD_DIM), F32)
            for f in range(frames):
                for j in range(spans):
                    block = jnp.where((row == f) & (col == j), offsets[f, j].astype(F32), block)
                block = jnp.where((row == f) & (col == spans), flags[f].astype(F32), block)
            scratch[0][...] = block.astype(BF16)
            for k in range(GROUP):
                pairs.append((scratch[0], outs[k].at[2 * frames, :, pl.ds(frames * HEAD_DIM, HEAD_DIM)]))
        move(pairs, sems)

    shape = (2 * frames + (1 if lead else 0), toks, width)
    return run(
        kernel,
        "pack_pair",
        [keys, values, *lead[:1]],
        [rows(shape)] * GROUP,
        [pltpu.VMEM((toks, HEAD_DIM), BF16)] if lead else [],
        GROUP * (2 + (frames + 1 if lead else 0)),
        [me, *lead[1:]],
        where=HBM,
    )


def pack_one(me, array, weight, gain, quarter, first, width):
    frames, toks, _ = array.shape

    def kernel(scalars, ins, outs, scratch, sems):
        mine = scalars[0][0]
        pairs = [(ins[0].at[:, :, lanes(mine ^ k, quarter, first, width)], outs[k]) for k in (1, 2, 3, 0)]
        for i in (1, 2):
            pairs.append((ins[i].at[:, lanes(mine, quarter, first, width)], outs[GROUP - 1 + i]))
        move(pairs, sems)

    outs = [rows((frames, toks, width))] * GROUP + [rows((weight.shape[0], width)), rows((1, width), F32)]
    return run(kernel, "pack_one", [array, weight, gain], outs, [], GROUP + 2, [me], where=HBM)


def edges(me, parts):
    def kernel(scalars, ins, outs, scratch, sems):
        mine = scalars[0][0]
        for out, owner in zip(outs, (GROUP - 1, 0)):
            for k in range(GROUP):

                @pl.when((mine ^ k) == owner)
                def _(out=out, k=k):
                    out[...] = ins[k][...]

    shape = rows(parts[0].shape)
    return run(kernel, "edges", parts, [shape, shape], [], 0, [me], us=0.2)


def attend(jobs):
    scores = [
        lax.dot_general(query, keys, (((1,), (1,)), ((), ())), preferred_element_type=F32) * HEAD_DIM ** (-0.5)
        for query, keys, _ in jobs
    ]
    tops = [jnp.max(x, axis=1, keepdims=True) for x in scores]
    scores = [jnp.exp(x - top) for x, top in zip(scores, tops)]
    scales = [1.0 / jnp.sum(x, axis=1, keepdims=True) for x in scores]
    weights = [(x * scale).astype(BF16) for x, scale in zip(scores, scales)]
    return [
        jnp.dot(w, values, preferred_element_type=F32).astype(BF16) for w, (_, _, values) in zip(weights, jobs)
    ]


def band(ref, spots, cols):
    return jnp.concatenate([ref[s, :, cols] for s in spots], axis=0)


def hint_branch(me, pairs_in, queries, before, after, weight, gain, setting, spans):
    frames, toks, width = queries[0].shape
    lead = setting is None
    total, wide = GROUP * frames, GROUP * frames + 2 * BAND
    heads = [slice(h * HEAD_DIM, (h + 1) * HEAD_DIM) for h in range(width // HEAD_DIM)]

    def kernel(scalars, ins, outs, scratch, sems):
        mine = scalars[0][0]
        kv, qs, (prev, following, w_ref, g_ref) = ins[:GROUP], ins[GROUP : 2 * GROUP], ins[2 * GROUP : 2 * GROUP + 4]
        mixed, up, down, keys_out = outs[:4]
        q_s, k_s, c_s = scratch[:3]
        if lead:
            pose_out, meta_out = outs[4:]
            meta = scratch[3]
            for k in range(GROUP):
                block = kv[k][2 * frames, : 2 * META, frames * HEAD_DIM : (frames + 1) * HEAD_DIM]
                meta_out[mine ^ k] = block.astype(F32).astype(I32)[:META]
            known = pltpu.make_async_copy(meta_out, meta, sems.at[0])
            known.start()
        else:
            meta = scalars[1]
        for k, src in enumerate([*kv, prev, following]):
            at = BAND + (mine ^ k) * frames if k < GROUP else (0 if k == GROUP else BAND + total)
            if lead:
                patches = [src[2 * frames, :, f * HEAD_DIM : (f + 1) * HEAD_DIM] for f in range(frames)]
                for f in range(frames):
                    pose_out[at + f] = patches[f]
            else:
                patches = [ins[-1][at + f] for f in range(frames)]
            hint = jnp.dot(jnp.concatenate(patches, axis=0), w_ref[...], preferred_element_type=F32)
            hint = hint.astype(BF16).astype(F32)
            for f in range(frames):
                own = hint[f * toks : (f + 1) * toks]
                keys_out[at + f] = src[f]
                k_s[at + f] = (src[f].astype(F32) + own).astype(BF16)
                c_s[at + f] = (src[frames + f].astype(F32) + own).astype(BF16)
                if k < GROUP:
                    q_s[k * frames + f] = (qs[k][f].astype(F32) + own).astype(BF16)
        if lead:
            known.wait()
        for k in range(GROUP):
            s = mine ^ k
            at, jobs = [], []
            for r in range(frames):
                f = s * frames + r
                spots = [BAND + f + meta[s, r, j] for j in range(spans)]
                for cols in heads:
                    at.append((r, meta[s, r, spans].astype(F32), cols))
                    jobs.append((q_s[k * frames + r, :, cols], band(k_s, spots, cols), band(c_s, spots, cols)))
            for (r, flag, cols), out in zip(at, attend(jobs)):
                residual = (flag * g_ref[:, cols] * out.astype(F32)).astype(BF16)
                plain = kv[k][frames + r, :, cols].astype(F32)
                mixed[s * frames + r, :, cols] = (plain + residual.astype(F32)).astype(BF16)
        up[...] = mixed[total - BAND :]
        down[...] = mixed[:BAND]

    outs = [rows((total, toks, width)), rows((BAND, toks, width)), rows((BAND, toks, width)), rows((wide, toks, width))]
    scratch = [
        pltpu.VMEM((total, toks, width), BF16),
        pltpu.VMEM((wide, toks, width), BF16),
        pltpu.VMEM((wide, toks, width), BF16),
    ]
    ins = [*pairs_in, *queries, before, after, weight, gain]
    scalars = [me]
    if lead:
        outs += [rows((wide, toks, HEAD_DIM)), rows((GROUP, META, HEAD_DIM), I32)]
        scratch.append(pltpu.SMEM((GROUP, META, HEAD_DIM), I32))
    else:
        ins.append(setting[0])
        scalars.append(setting[1])
    return run(kernel, "hint_branch", ins, outs, scratch, 1, scalars, us=1.2 * len(heads))


def base_block(me, queries, keys, mixed, mixed_before, mixed_after, meta, spans):
    frames, toks, width = queries[0].shape
    total, wide = GROUP * frames, GROUP * frames + 2 * BAND
    heads = [slice(h * HEAD_DIM, (h + 1) * HEAD_DIM) for h in range(width // HEAD_DIM)]

    def kernel(scalars, ins, outs, scratch, sems):
        mine, meta = scalars[0][0], scalars[1]
        qs, k_ref, m_s = ins[:GROUP], ins[GROUP], scratch[0]
        m_s[BAND : BAND + total] = ins[GROUP + 1][...]
        m_s[:BAND] = ins[GROUP + 2][...]
        m_s[BAND + total :] = ins[GROUP + 3][...]
        for k in range(GROUP):
            s = mine ^ k
            at, jobs = [], []
            for r in range(frames):
                spots = [BAND + s * frames + r + meta[s, r, j] for j in range(spans)]
                for cols in heads:
                    at.append((r, cols))
                    jobs.append((qs[k][r, :, cols], band(k_ref, spots, cols), band(m_s, spots, cols)))
            for (r, cols), out in zip(at, attend(jobs)):
                outs[k][r, :, cols] = out

    ins = [*queries, keys, mixed, mixed_before, mixed_after]
    scratch = [pltpu.VMEM((wide, toks, width), BF16)]
    outs = [rows((frames, toks, width))] * GROUP
    return run(kernel, "base_block", ins, outs, scratch, 0, [me, meta], us=0.8 * len(heads))


def place(me, parts, into, model_width, quarter, first):
    frames, toks, width = parts[0].shape

    def kernel(scalars, ins, outs, scratch, sems):
        mine = scalars[0][0]
        move([(ins[k], outs[0].at[:, :, lanes(mine ^ k, quarter, first, width)]) for k in range(GROUP)], sems)

    held = [] if into is None else [into]
    return run(
        kernel,
        "place",
        [*parts, *held],
        [rows((frames, toks, model_width))],
        [],
        GROUP,
        [me],
        where=[VMEM] * GROUP + [HBM] * len(held),
        to=HBM,
        aliases={} if into is None else {1 + GROUP: 0},
        us=0.8,
    )[0]


def solution(mesh):
    count = mesh.shape["tm"]
    assert count % GROUP == 0
    across = [[(i, i ^ k) for i in range(count)] for k in range(GROUP)]
    upward = [(i, (i + GROUP) % count) for i in range(count)]
    downward = [(i, (i - GROUP) % count) for i in range(count)]

    def exchange(parts):
        return [parts[0]] + [lax.ppermute(parts[k], "tm", across[k]) for k in range(1, GROUP)]

    def body(queries, key_states, value_states, pose_depth, hint_weight, control_gain, band_offsets, control_flags):
        frames, _, model_width = queries.shape
        spans = band_offsets.shape[1]
        quarter = model_width // GROUP
        assert frames == BAND and sum(SLICES) * HEAD_DIM == quarter
        me = lax.rem(lax.axis_index("tm"), GROUP).astype(I32).reshape(1)
        gain = control_gain.reshape(1, -1)
        cuts = [(sum(SLICES[:c]) * HEAD_DIM, n * HEAD_DIM) for c, n in enumerate(SLICES)]
        wires = {"y": [], "z": []}

        def after(values, *deps):
            deps = [d for d in deps if d is not None]
            if not deps:
                return values
            return lax.optimization_barrier((values, deps))[0]

        def held(wire, depth):
            return wires[wire][-depth] if len(wires[wire]) >= depth else None

        def across_group(parts):
            sent = after(parts[1:], held("y", DEPTH_Y))
            got = [lax.ppermute(p, "tm", across[k + 1]) for k, p in enumerate(sent)]
            wires["y"].append(got[-1])
            return [parts[0], *got]

        def along(last, start):
            last, start = after([last, start], held("z", DEPTH_Z))
            got = (lax.ppermute(last, "tm", upward), lax.ppermute(start, "tm", downward))
            wires["z"].append(got[-1])
            return got

        n = len(cuts)
        pairs, asked, shares, sides, mixed, parts = {}, {}, {}, {}, {}, {}
        state = {"setting": None, "out": None}

        def step(name, c):
            first, width = cuts[c]
            if name == "KV":
                lead = [pose_depth, band_offsets, control_flags] if c == 0 else []
                pairs[c] = across_group(pack_pair(me, key_states, value_states, lead, quarter, first, width))
            elif name == "Q":
                *sent, weight, share = pack_one(me, queries, hint_weight, gain, quarter, first, width)
                asked[c] = across_group(sent)
                shares[c] = (weight, share)
            elif name == "Z":
                sides[c] = along(*edges(me, pairs[c]))
            elif name == "H":
                got = hint_branch(me, pairs[c], asked[c], *sides[c], *shares[c], state["setting"], spans)
                if state["setting"] is None:
                    state["setting"] = got[4:]
                mixed[c] = (got[3], got[0], *along(got[1], got[2]))
            elif name == "B":
                parts[c] = across_group(base_block(me, asked[c], *mixed[c], state["setting"][1], spans))
            else:
                state["out"] = place(me, parts[c], state["out"], model_width, quarter, first)

        for name, c in ORDER:
            step(name, c)
        return state["out"]

    return jax.shard_map(
        body,
        mesh=mesh,
        in_specs=(
            P(("grp", "tm"), None, None),
            P(("grp", "tm"), None, None),
            P(("grp", "tm"), None, None),
            P(("grp", "tm"), None, None),
            P(),
            P(),
            P(("grp", "tm"), None),
            P(("grp", "tm")),
        ),
        out_specs=P(("grp", "tm"), None, None),
        check_vma=False,
    )
```

```python
import jax
import jax.numpy as jnp
from jax import lax
from jax.experimental import pallas as pl
from jax.experimental.pallas import tpu as pltpu
from jax.sharding import PartitionSpec as P

HEAD_DIM = 128
BAND = 2
GROUP = 4
SLICES = (5, 5)
META = 8
PIECE = 16
ORDER = [("KV", 0), ("C", 0), ("KV", 1), ("Z", 0), ("Q", 0), ("Z", 1), ("Q", 1), ("H", 0), ("H", 1), ("B", 0), ("B", 1), ("P", 0), ("P", 1)]
DEPTH_Y, DEPTH_Z = 3, 2
F32 = jnp.float32
BF16 = jnp.bfloat16
I32 = jnp.int32
VMEM = pl.BlockSpec(memory_space=pltpu.VMEM)
SMEM = pl.BlockSpec(memory_space=pltpu.SMEM)
HBM = pl.BlockSpec(memory_space=pltpu.HBM)


def run(kernel, name, ins, outs, scratch, copies, scalars=(), where=VMEM, to=VMEM, aliases=None, us=1.0):
    a, b, c, d = len(scalars), len(ins), len(outs), len(scratch)

    def body(*refs):
        kernel(refs[:a], refs[a : a + b], refs[a + b : a + b + c], refs[a + b + c : a + b + c + d], refs[-1])

    return pl.pallas_call(
        body,
        out_shape=list(outs),
        in_specs=[SMEM] * a + (where if isinstance(where, list) else [where] * b),
        out_specs=[to] * c,
        scratch_shapes=[*scratch, pltpu.SemaphoreType.DMA((max(copies, 1),))],
        input_output_aliases=aliases or {},
        compiler_params=pltpu.CompilerParams(vmem_limit_bytes=16 * 1024 * 1024),
        cost_estimate=pl.CostEstimate(flops=1, bytes_accessed=int(us * 3.4e6), transcendentals=0),
        name=name,
    )(*scalars, *ins)


def move(pairs, sems):
    copies = [pltpu.make_async_copy(s, d, sems.at[i]) for i, (s, d) in enumerate(pairs)]
    for copy in copies:
        copy.start()
    for copy in copies:
        copy.wait()


def lanes(me, quarter, first, width):
    return pl.ds(pl.multiple_of(me * quarter + first, HEAD_DIM), width)


def rows(shape, dtype=BF16):
    return jax.ShapeDtypeStruct(shape, dtype)


def notes_at(i, width):
    blocks = width // HEAD_DIM
    return PIECE * (i // blocks), HEAD_DIM * (i % blocks)


def note_rows(pieces, width):
    return PIECE * -(-pieces * HEAD_DIM // width)


def read_note(ref, top, left, width, i):
    down, right = notes_at(i, width)
    return ref[top + down : top + down + PIECE, left + right : left + right + HEAD_DIM]


def pack(me, ks, arrays, notes, quarter, first, width):
    frames, toks, _ = arrays[0].shape
    size = frames * toks
    pieces = size // PIECE + 1 if notes else 0
    base = len(arrays) * size

    def kernel(scalars, ins, outs, scratch, sems):
        mine = scalars[0][0]
        pairs = list(zip(ins[len(arrays) :], scratch))
        for i, k in enumerate(ks):
            where = lanes(mine ^ k, quarter, first, width)
            for j in range(len(arrays)):
                for f in range(frames):
                    pairs.append((ins[j].at[f, :, where], outs[i].at[pl.ds(j * size + f * toks, toks)]))
        copies = [pltpu.make_async_copy(s, d, sems.at[i]) for i, (s, d) in enumerate(pairs)]
        for copy in copies:
            copy.start()
        if notes:
            for copy in copies[: len(notes)]:
                copy.wait()
            patches, offsets, flags = scratch
            spans = offsets.shape[1]
            row = lax.broadcasted_iota(I32, (PIECE, HEAD_DIM), 0)
            col = lax.broadcasted_iota(I32, (PIECE, HEAD_DIM), 1)
            block = jnp.zeros((PIECE, HEAD_DIM), F32)
            for f in range(frames):
                for j in range(spans):
                    block = jnp.where((row == f) & (col == j), offsets[f, j].astype(F32), block)
                block = jnp.where((row == f) & (col == spans), flags[f].astype(F32), block)
            per = toks // PIECE
            for i in range(pieces):
                top, left = notes_at(i, width)
                if i == pieces - 1:
                    piece = block.astype(BF16)
                else:
                    piece = patches[i // per, PIECE * (i % per) : PIECE * (i % per + 1)]
                for out in outs:
                    out[base + top : base + top + PIECE, left : left + HEAD_DIM] = piece
        for copy in copies[len(notes) :]:
            copy.wait()

    scratch = []
    if notes:
        pose, offsets, flags = notes
        scratch = [pltpu.VMEM(pose.shape, BF16), pltpu.SMEM(offsets.shape, I32), pltpu.SMEM(flags.shape, I32)]
    outs = [rows((base + note_rows(pieces, width), width))] * len(ks)
    copies = frames * len(arrays) * len(ks) + len(notes)
    return run(kernel, "pack", [*arrays, *notes], outs, scratch, copies, [me], where=HBM)


def share_of(me, weight, gain, quarter):
    def kernel(scalars, ins, outs, scratch, sems):
        mine = scalars[0][0]
        move([(i.at[:, lanes(mine, quarter, 0, quarter)], o) for i, o in zip(ins, outs)], sems)

    outs = [rows((weight.shape[0], quarter)), rows((1, quarter), F32)]
    return run(kernel, "share", [weight, gain], outs, [], 2, [me], where=HBM)


def edges(me, near, far, size, first, width, lead):
    pieces = size // PIECE + 1 if lead else 0

    def kernel(scalars, ins, outs, scratch, sems):
        mine = scalars[0][0]
        for out, owner in zip(outs, (GROUP - 1, 0)):
            for k in range(GROUP):

                @pl.when((mine ^ k) == owner)
                def _(out=out, k=k):
                    if k >= 2:
                        out[...] = ins[k][...]
                    else:
                        out[: 2 * size] = ins[k][: 2 * size, first : first + width]
                        for i in range(pieces - 1):
                            top, left = notes_at(i, width)
                            top += 2 * size
                            piece = read_note(ins[k], 3 * size, 0, ins[k].shape[1], i)
                            out[top : top + PIECE, left : left + HEAD_DIM] = piece

    shape = rows(far[0].shape)
    return run(kernel, "edges", [*near, *far], [shape, shape], [], 0, [me], us=0.2)


def attend(jobs):
    scores = [
        lax.dot_general(query, keys, (((1,), (1,)), ((), ())), preferred_element_type=F32) * HEAD_DIM ** (-0.5)
        for query, keys, _ in jobs
    ]
    tops = [jnp.max(x, axis=1, keepdims=True) for x in scores]
    scores = [jnp.exp(x - top) for x, top in zip(scores, tops)]
    scales = [1.0 / jnp.sum(x, axis=1, keepdims=True) for x in scores]
    weights = [(x * scale).astype(BF16) for x, scale in zip(scores, scales)]
    return [
        jnp.dot(w, values, preferred_element_type=F32).astype(BF16) for w, (_, _, values) in zip(weights, jobs)
    ]


def band(ref, spots, cols):
    return jnp.concatenate([ref[s, :, cols] for s in spots], axis=0)


def hint_branch(me, near, pairs, queries, before, after, weight, gain, setting, spans, frames, first):
    size, width = queries[0].shape
    toks = size // frames
    lead = setting is None
    total, wide = GROUP * frames, GROUP * frames + 2 * BAND
    heads = [slice(h * HEAD_DIM, (h + 1) * HEAD_DIM) for h in range(width // HEAD_DIM)]
    own_lanes = slice(first, first + width)

    def kernel(scalars, ins, outs, scratch, sems):
        mine = scalars[0][0]
        kv, qs = ins[:GROUP], ins[GROUP : GROUP + 2]
        prev, following, w_ref, g_ref = ins[GROUP + 2 : GROUP + 6]
        mixed, up, down, keys_out = outs[:4]
        q_s, k_s, c_s = scratch[:3]
        pieces, per = size // PIECE, toks // PIECE

        def taken(k, j, f):
            if k < 2:
                top = j * size + f * toks
                return ins[k][top : top + toks, own_lanes]
            if j == 2:
                return qs[k - 2][f * toks : (f + 1) * toks]
            src = kv[k] if k < GROUP else (prev, following)[k - GROUP]
            return src[j * size + f * toks : j * size + (f + 1) * toks]

        def note(k, i):
            if k < 2:
                return read_note(ins[k], 3 * size, 0, ins[k].shape[1], i)
            src = kv[k] if k < GROUP else (prev, following)[k - GROUP]
            return read_note(src, 2 * size, 0, width, i)

        if lead:
            pose_out, meta_out = outs[4:]
            meta = scratch[3]
            for k in range(GROUP):
                meta_out[mine ^ k] = note(k, pieces).astype(F32).astype(I32)[:META]
            known = pltpu.make_async_copy(meta_out, meta, sems.at[0])
            known.start()
        else:
            meta = scalars[1]
        for k in range(GROUP + 2):
            at = BAND + (mine ^ k) * frames if k < GROUP else (0 if k == GROUP else BAND + total)
            if lead:
                patches = [jnp.concatenate([note(k, f * per + i) for i in range(per)], axis=0) for f in range(frames)]
                for f in range(frames):
                    pose_out[at + f] = patches[f]
            else:
                patches = [ins[-1][at + f] for f in range(frames)]
            hint = jnp.dot(jnp.concatenate(patches, axis=0), w_ref[:, own_lanes], preferred_element_type=F32)
            hint = hint.astype(BF16).astype(F32)
            for f in range(frames):
                own = hint[f * toks : (f + 1) * toks]
                key = taken(k, 0, f)
                keys_out[at + f] = key
                k_s[at + f] = (key.astype(F32) + own).astype(BF16)
                c_s[at + f] = (taken(k, 1, f).astype(F32) + own).astype(BF16)
                if k < GROUP:
                    q_s[k * frames + f] = (taken(k, 2, f).astype(F32) + own).astype(BF16)
        if lead:
            known.wait()
        for k in range(GROUP):
            s = mine ^ k
            at, jobs = [], []
            for r in range(frames):
                f = s * frames + r
                spots = [BAND + f + meta[s, r, j] for j in range(spans)]
                for cols in heads:
                    at.append((r, meta[s, r, spans].astype(F32), cols))
                    jobs.append((q_s[k * frames + r, :, cols], band(k_s, spots, cols), band(c_s, spots, cols)))
            for (r, flag, cols), out in zip(at, attend(jobs)):
                scale = g_ref[:, first + cols.start : first + cols.stop]
                residual = (flag * scale * out.astype(F32)).astype(BF16)
                plain = taken(k, 1, r)[:, cols].astype(F32)
                mixed[s * frames + r, :, cols] = (plain + residual.astype(F32)).astype(BF16)
        up[...] = mixed[total - BAND :]
        down[...] = mixed[:BAND]

    outs = [rows((total, toks, width)), rows((BAND, toks, width)), rows((BAND, toks, width)), rows((wide, toks, width))]
    scratch = [
        pltpu.VMEM((total, toks, width), BF16),
        pltpu.VMEM((wide, toks, width), BF16),
        pltpu.VMEM((wide, toks, width), BF16),
    ]
    ins = [*near, *pairs, *queries, before, after, weight, gain]
    scalars = [me]
    if lead:
        outs += [rows((wide, toks, HEAD_DIM)), rows((GROUP, META, HEAD_DIM), I32)]
        scratch.append(pltpu.SMEM((GROUP, META, HEAD_DIM), I32))
    else:
        ins.append(setting[0])
        scalars.append(setting[1])
    return run(kernel, "hint_branch", ins, outs, scratch, 1, scalars, us=0.5 + 0.8 * len(heads))


def base_block(me, near, queries, keys, mixed, mixed_before, mixed_after, meta, spans, first):
    total, toks, width = mixed.shape
    frames, wide = total // GROUP, total + 2 * BAND
    size = frames * toks
    heads = [slice(h * HEAD_DIM, (h + 1) * HEAD_DIM) for h in range(width // HEAD_DIM)]

    def kernel(scalars, ins, outs, scratch, sems):
        mine, meta = scalars[0][0], scalars[1]
        k_ref, m_s = ins[GROUP], scratch[0]
        m_s[BAND : BAND + total] = ins[GROUP + 1][...]
        m_s[:BAND] = ins[GROUP + 2][...]
        m_s[BAND + total :] = ins[GROUP + 3][...]
        for k in range(GROUP):
            s = mine ^ k
            at, jobs = [], []
            for r in range(frames):
                spots = [BAND + s * frames + r + meta[s, r, j] for j in range(spans)]
                for cols in heads:
                    at.append((r, cols))
                    if k < 2:
                        top = 2 * size + r * toks
                        query = ins[k][top : top + toks, first + cols.start : first + cols.stop]
                    else:
                        query = ins[k][r * toks : (r + 1) * toks, cols]
                    jobs.append((query, band(k_ref, spots, cols), band(m_s, spots, cols)))
            for (r, cols), out in zip(at, attend(jobs)):
                outs[k][r, :, cols] = out

    ins = [*near, *queries, keys, mixed, mixed_before, mixed_after]
    scratch = [pltpu.VMEM((wide, toks, width), BF16)]
    outs = [rows((frames, toks, width))] * GROUP
    return run(kernel, "base_block", ins, outs, scratch, 0, [me, meta], us=0.7 * len(heads))


def place(me, parts, into, model_width, quarter, first):
    frames, toks, width = parts[0].shape

    def kernel(scalars, ins, outs, scratch, sems):
        mine = scalars[0][0]
        move([(ins[k], outs[0].at[:, :, lanes(mine ^ k, quarter, first, width)]) for k in range(GROUP)], sems)

    held = [] if into is None else [into]
    return run(
        kernel,
        "place",
        [*parts, *held],
        [rows((frames, toks, model_width))],
        [],
        GROUP,
        [me],
        where=[VMEM] * GROUP + [HBM] * len(held),
        to=HBM,
        aliases={} if into is None else {1 + GROUP: 0},
        us=0.8,
    )[0]


def solution(mesh):
    count = mesh.shape["tm"]
    assert count % GROUP == 0
    across = [[(i, i ^ k) for i in range(count)] for k in range(GROUP)]
    upward = [(i, (i + GROUP) % count) for i in range(count)]
    downward = [(i, (i - GROUP) % count) for i in range(count)]

    def exchange(parts):
        return [parts[0]] + [lax.ppermute(parts[k], "tm", across[k]) for k in range(1, GROUP)]

    def body(queries, key_states, value_states, pose_depth, hint_weight, control_gain, band_offsets, control_flags):
        frames, _, model_width = queries.shape
        spans = band_offsets.shape[1]
        quarter = model_width // GROUP
        assert frames == BAND and sum(SLICES) * HEAD_DIM == quarter
        me = lax.rem(lax.axis_index("tm"), GROUP).astype(I32).reshape(1)
        gain = control_gain.reshape(1, -1)
        queries, key_states, value_states, pose_depth, hint_weight, gain, band_offsets, control_flags = [
            pltpu.with_memory_space_constraint(a, pltpu.HBM)
            for a in (
                queries, key_states, value_states, pose_depth, hint_weight, gain, band_offsets, control_flags
            )
        ]
        cuts = [(sum(SLICES[:c]) * HEAD_DIM, n * HEAD_DIM) for c, n in enumerate(SLICES)]
        wires = {"y": [], "z": []}

        def after(values, wire, depth):
            if len(wires[wire]) < depth:
                return values
            return lax.optimization_barrier((values, wires[wire][-depth]))[0]

        def far_group(parts):
            got = []
            for part, k in zip(parts, (3, 2)):
                part = after(part, "y", DEPTH_Y)
                got.append(lax.ppermute(part, "tm", across[k]))
                wires["y"].append(got[-1])
            return [got[1], got[0]]

        def along(last, start):
            last, start = after([last, start], "z", DEPTH_Z)
            got = (lax.ppermute(last, "tm", upward), lax.ppermute(start, "tm", downward))
            wires["z"].append(got)
            return got

        size = frames * queries.shape[1]
        notes = [pose_depth, band_offsets, control_flags]
        pairs, asked, sides, mixed, parts = {}, {}, {}, {}, {}
        state = {"setting": None, "out": None}

        def step(name, c):
            first, width = cuts[c]
            if name == "KV":
                sent = pack(me, (3, 2), [key_states, value_states], notes if c == 0 else [], quarter, first, width)
                pairs[c] = far_group(sent)
            elif name == "C":
                mine, other = pack(me, (0, 1), [key_states, value_states, queries], notes, quarter, 0, quarter)
                state["near"] = [mine, lax.ppermute(other, "tm", across[1])]
                state["shares"] = share_of(me, hint_weight, gain, quarter)
            elif name == "Q":
                asked[c] = far_group(pack(me, (3, 2), [queries], [], quarter, first, width))
            elif name == "Z":
                sides[c] = along(*edges(me, state["near"], pairs[c], size, first, width, c == 0))
            elif name == "H":
                got = hint_branch(
                    me, state["near"], pairs[c], asked[c], *sides[c], *state["shares"], state["setting"], spans, frames, first
                )
                if state["setting"] is None:
                    state["setting"] = got[4:]
                mixed[c] = (got[3], got[0], *along(got[1], got[2]))
            elif name == "B":
                mine, other, *far = base_block(
                    me, state["near"], asked[c], *mixed[c], state["setting"][1], spans, first
                )
                far = far_group(far[::-1])
                parts[c] = [mine, lax.ppermute(other, "tm", across[1]), *far]
            else:
                state["out"] = place(me, parts[c], state["out"], model_width, quarter, first)

        for name, c in ORDER:
            step(name, c)
        return state["out"]

    return jax.shard_map(
        body,
        mesh=mesh,
        in_specs=(
            P(("grp", "tm"), None, None),
            P(("grp", "tm"), None, None),
            P(("grp", "tm"), None, None),
            P(("grp", "tm"), None, None),
            P(),
            P(),
            P(("grp", "tm"), None),
            P(("grp", "tm")),
        ),
        out_specs=P(("grp", "tm"), None, None),
        check_vma=False,
    )
```

```python
import jax
import jax.numpy as jnp
from jax import lax
from jax.experimental import pallas as pl
from jax.experimental.pallas import tpu as pltpu
from jax.sharding import PartitionSpec as P

HEAD_DIM = 128
BAND = 2
GROUP = 4
SLICES = (5, 5)
META = 8
PIECE = 16
F32 = jnp.float32
BF16 = jnp.bfloat16
I32 = jnp.int32
VMEM = pl.BlockSpec(memory_space=pltpu.VMEM)
SMEM = pl.BlockSpec(memory_space=pltpu.SMEM)
HBM = pl.BlockSpec(memory_space=pltpu.HBM)


def run(kernel, name, ins, outs, scratch, copies, scalars=(), where=VMEM, to=VMEM, aliases=None, us=1.0):
    a, b, c, d = len(scalars), len(ins), len(outs), len(scratch)

    def body(*refs):
        kernel(refs[:a], refs[a : a + b], refs[a + b : a + b + c], refs[a + b + c : a + b + c + d], refs[-1])

    return pl.pallas_call(
        body,
        out_shape=list(outs),
        in_specs=[SMEM] * a + (where if isinstance(where, list) else [where] * b),
        out_specs=[to] * c,
        scratch_shapes=[*scratch, pltpu.SemaphoreType.DMA((max(copies, 1),))],
        input_output_aliases=aliases or {},
        compiler_params=pltpu.CompilerParams(vmem_limit_bytes=16 * 1024 * 1024),
        cost_estimate=pl.CostEstimate(flops=1, bytes_accessed=int(us * 3.4e6), transcendentals=0),
        name=name,
    )(*scalars, *ins)


def move(pairs, sems):
    copies = [pltpu.make_async_copy(s, d, sems.at[i]) for i, (s, d) in enumerate(pairs)]
    for copy in copies:
        copy.start()
    for copy in copies:
        copy.wait()


def lanes(me, quarter, first, width):
    return pl.ds(pl.multiple_of(me * quarter + first, HEAD_DIM), width)


def rows(shape, dtype=BF16):
    return jax.ShapeDtypeStruct(shape, dtype)


def notes_at(i, width):
    blocks = width // HEAD_DIM
    return PIECE * (i // blocks), HEAD_DIM * (i % blocks)


def note_rows(pieces, width):
    return PIECE * -(-pieces * HEAD_DIM // width)


def read_note(ref, top, left, width, i):
    down, right = notes_at(i, width)
    return ref[top + down : top + down + PIECE, left + right : left + right + HEAD_DIM]


def pack(me, ks, arrays, notes, quarter, first, width):
    frames, toks, _ = arrays[0].shape
    size = frames * toks
    pieces = size // PIECE + 1 if notes else 0
    base = len(arrays) * size

    def kernel(scalars, ins, outs, scratch, sems):
        mine = scalars[0][0]
        pairs = list(zip(ins[len(arrays) :], scratch))
        for i, k in enumerate(ks):
            where = lanes(mine ^ k, quarter, first, width)
            for j in range(len(arrays)):
                for f in range(frames):
                    pairs.append((ins[j].at[f, :, where], outs[i].at[pl.ds(j * size + f * toks, toks)]))
        copies = [pltpu.make_async_copy(s, d, sems.at[i]) for i, (s, d) in enumerate(pairs)]
        for copy in copies:
            copy.start()
        if notes:
            for copy in copies[: len(notes)]:
                copy.wait()
            patches, offsets, flags = scratch
            spans = offsets.shape[1]
            row = lax.broadcasted_iota(I32, (PIECE, HEAD_DIM), 0)
            col = lax.broadcasted_iota(I32, (PIECE, HEAD_DIM), 1)
            block = jnp.zeros((PIECE, HEAD_DIM), F32)
            for f in range(frames):
                for j in range(spans):
                    block = jnp.where((row == f) & (col == j), offsets[f, j].astype(F32), block)
                block = jnp.where((row == f) & (col == spans), flags[f].astype(F32), block)
            per = toks // PIECE
            for i in range(pieces):
                top, left = notes_at(i, width)
                if i == pieces - 1:
                    piece = block.astype(BF16)
                else:
                    piece = patches[i // per, PIECE * (i % per) : PIECE * (i % per + 1)]
                for out in outs:
                    out[base + top : base + top + PIECE, left : left + HEAD_DIM] = piece
        for copy in copies[len(notes) :]:
            copy.wait()

    scratch = []
    if notes:
        pose, offsets, flags = notes
        scratch = [pltpu.VMEM(pose.shape, BF16), pltpu.SMEM(offsets.shape, I32), pltpu.SMEM(flags.shape, I32)]
    outs = [rows((base + note_rows(pieces, width), width))] * len(ks)
    copies = frames * len(arrays) * len(ks) + len(notes)
    return run(kernel, "pack", [*arrays, *notes], outs, scratch, copies, [me], where=HBM)


def pack_own(me, queries, weight, gain, quarter):
    frames, toks, _ = queries.shape

    def kernel(scalars, ins, outs, scratch, sems):
        mine = scalars[0][0]
        pairs = []
        for k in range(2):
            for f in range(frames):
                where = lanes(mine ^ k, quarter, 0, quarter)
                pairs.append((ins[0].at[f, :, where], outs[k].at[pl.ds(f * toks, toks)]))
        for i in (1, 2):
            pairs.append((ins[i].at[:, lanes(mine, quarter, 0, quarter)], outs[1 + i]))
        move(pairs, sems)

    outs = [rows((frames * toks, quarter))] * 2 + [rows((weight.shape[0], quarter)), rows((1, quarter), F32)]
    return run(kernel, "pack_own", [queries, weight, gain], outs, [], 2 * frames + 2, [me], where=HBM)


def edges(me, parts):
    def kernel(scalars, ins, outs, scratch, sems):
        mine = scalars[0][0]
        for out, owner in zip(outs, (GROUP - 1, 0)):
            for k in range(GROUP):

                @pl.when((mine ^ k) == owner)
                def _(out=out, k=k):
                    out[...] = ins[k][...]

    shape = rows(parts[0].shape)
    return run(kernel, "edges", parts, [shape, shape], [], 0, [me], us=0.2)


def attend(jobs):
    scores = [
        lax.dot_general(query, keys, (((1,), (1,)), ((), ())), preferred_element_type=F32) * HEAD_DIM ** (-0.5)
        for query, keys, _ in jobs
    ]
    tops = [jnp.max(x, axis=1, keepdims=True) for x in scores]
    scores = [jnp.exp(x - top) for x, top in zip(scores, tops)]
    scales = [1.0 / jnp.sum(x, axis=1, keepdims=True) for x in scores]
    weights = [(x * scale).astype(BF16) for x, scale in zip(scores, scales)]
    return [
        jnp.dot(w, values, preferred_element_type=F32).astype(BF16) for w, (_, _, values) in zip(weights, jobs)
    ]


def band(ref, spots, cols):
    return jnp.concatenate([ref[s, :, cols] for s in spots], axis=0)


def hint_branch(me, pairs, queries, before, after, weight, gain, setting, spans, frames, first):
    size, width = queries[-1].shape
    toks = size // frames
    lead = setting is None
    total, wide = GROUP * frames, GROUP * frames + 2 * BAND
    heads = [slice(h * HEAD_DIM, (h + 1) * HEAD_DIM) for h in range(width // HEAD_DIM)]
    own_lanes = slice(first, first + width)

    def kernel(scalars, ins, outs, scratch, sems):
        mine = scalars[0][0]
        sources, qs = [*ins[:GROUP], *ins[2 * GROUP : 2 * GROUP + 2]], ins[GROUP : 2 * GROUP]
        w_ref, g_ref = ins[2 * GROUP + 2 : 2 * GROUP + 4]
        mixed, up, down, keys_out = outs[:4]
        q_s, k_s, c_s = scratch[:3]
        pieces, per = size // PIECE, toks // PIECE

        def taken(k, j, f):
            if j < 2:
                return sources[k][j * size + f * toks : j * size + (f + 1) * toks]
            return qs[k][f * toks : (f + 1) * toks, own_lanes if k < 2 else slice(None)]

        def note(k, i):
            return read_note(sources[k], 2 * size, 0, width, i)

        if lead:
            pose_out, meta_out = outs[4:]
            meta = scratch[3]
            for k in range(GROUP):
                meta_out[mine ^ k] = note(k, pieces).astype(F32).astype(I32)[:META]
            known = pltpu.make_async_copy(meta_out, meta, sems.at[0])
            known.start()
        else:
            meta = scalars[1]
        for k in range(GROUP + 2):
            at = BAND + (mine ^ k) * frames if k < GROUP else (0 if k == GROUP else BAND + total)
            if lead:
                patches = [jnp.concatenate([note(k, f * per + i) for i in range(per)], axis=0) for f in range(frames)]
                for f in range(frames):
                    pose_out[at + f] = patches[f]
            else:
                patches = [ins[-1][at + f] for f in range(frames)]
            hint = jnp.dot(jnp.concatenate(patches, axis=0), w_ref[:, own_lanes], preferred_element_type=F32)
            hint = hint.astype(BF16).astype(F32)
            for f in range(frames):
                own = hint[f * toks : (f + 1) * toks]
                key = taken(k, 0, f)
                keys_out[at + f] = key
                k_s[at + f] = (key.astype(F32) + own).astype(BF16)
                c_s[at + f] = (taken(k, 1, f).astype(F32) + own).astype(BF16)
                if k < GROUP:
                    q_s[k * frames + f] = (taken(k, 2, f).astype(F32) + own).astype(BF16)
        if lead:
            known.wait()
        at, jobs = [], []
        for k in range(GROUP):
            for r in range(frames):
                s = mine ^ k
                f = s * frames + r
                spots = [BAND + f + meta[s, r, j] for j in range(spans)]
                for cols in heads:
                    at.append((k, r, f, meta[s, r, spans].astype(F32), cols))
                    jobs.append((q_s[k * frames + r, :, cols], band(k_s, spots, cols), band(c_s, spots, cols)))
        for (k, r, f, flag, cols), out in zip(at, attend(jobs)):
            scale = g_ref[:, first + cols.start : first + cols.stop]
            residual = (flag * scale * out.astype(F32)).astype(BF16)
            mixed[f, :, cols] = (taken(k, 1, r)[:, cols].astype(F32) + residual.astype(F32)).astype(BF16)
        up[...] = mixed[total - BAND :]
        down[...] = mixed[:BAND]

    outs = [rows((total, toks, width)), rows((BAND, toks, width)), rows((BAND, toks, width)), rows((wide, toks, width))]
    scratch = [
        pltpu.VMEM((total, toks, width), BF16),
        pltpu.VMEM((wide, toks, width), BF16),
        pltpu.VMEM((wide, toks, width), BF16),
    ]
    ins = [*pairs, *queries, before, after, weight, gain]
    scalars = [me]
    if lead:
        outs += [rows((wide, toks, HEAD_DIM)), rows((GROUP, META, HEAD_DIM), I32)]
        scratch.append(pltpu.SMEM((GROUP, META, HEAD_DIM), I32))
    else:
        ins.append(setting[0])
        scalars.append(setting[1])
    return run(kernel, "hint_branch", ins, outs, scratch, 1, scalars, us=0.5 + 0.8 * len(heads))


def base_block(me, queries, keys, mixed, mixed_before, mixed_after, meta, spans, first):
    total, toks, width = mixed.shape
    frames, wide = total // GROUP, total + 2 * BAND
    heads = [slice(h * HEAD_DIM, (h + 1) * HEAD_DIM) for h in range(width // HEAD_DIM)]

    def kernel(scalars, ins, outs, scratch, sems):
        mine, meta = scalars[0][0], scalars[1]
        k_ref, m_s = ins[GROUP], scratch[0]
        m_s[BAND : BAND + total] = ins[GROUP + 1][...]
        m_s[:BAND] = ins[GROUP + 2][...]
        m_s[BAND + total :] = ins[GROUP + 3][...]
        at, jobs = [], []
        for k in range(GROUP):
            for r in range(frames):
                s = mine ^ k
                spots = [BAND + s * frames + r + meta[s, r, j] for j in range(spans)]
                for cols in heads:
                    at.append((k, r, cols))
                    left = first if k < 2 else 0
                    query = ins[k][r * toks : (r + 1) * toks, left + cols.start : left + cols.stop]
                    jobs.append((query, band(k_ref, spots, cols), band(m_s, spots, cols)))
        for (k, r, cols), out in zip(at, attend(jobs)):
            outs[k][r, :, cols] = out

    ins = [*queries, keys, mixed, mixed_before, mixed_after]
    scratch = [pltpu.VMEM((wide, toks, width), BF16)]
    outs = [rows((frames, toks, width))] * GROUP
    return run(kernel, "base_block", ins, outs, scratch, 0, [me, meta], us=0.7 * len(heads))


def place(me, parts, into, model_width, quarter, first):
    frames, toks, width = parts[0].shape

    def kernel(scalars, ins, outs, scratch, sems):
        mine = scalars[0][0]
        move([(ins[k], outs[0].at[:, :, lanes(mine ^ k, quarter, first, width)]) for k in range(GROUP)], sems)

    held = [] if into is None else [into]
    return run(
        kernel,
        "place",
        [*parts, *held],
        [rows((frames, toks, model_width))],
        [],
        GROUP,
        [me],
        where=[VMEM] * GROUP + [HBM] * len(held),
        to=HBM,
        aliases={} if into is None else {1 + GROUP: 0},
        us=0.8,
    )[0]


def solution(mesh):
    count = mesh.shape["tm"]
    assert count % GROUP == 0
    across = [[(i, i ^ k) for i in range(count)] for k in range(GROUP)]
    upward = [(i, (i + GROUP) % count) for i in range(count)]
    downward = [(i, (i - GROUP) % count) for i in range(count)]

    def exchange(parts):
        return [parts[0]] + [lax.ppermute(parts[k], "tm", across[k]) for k in range(1, GROUP)]

    def body(queries, key_states, value_states, pose_depth, hint_weight, control_gain, band_offsets, control_flags):
        frames, _, model_width = queries.shape
        spans = band_offsets.shape[1]
        quarter = model_width // GROUP
        assert frames == BAND and sum(SLICES) * HEAD_DIM == quarter
        me = lax.rem(lax.axis_index("tm"), GROUP).astype(I32).reshape(1)
        gain = control_gain.reshape(1, -1)
        queries, key_states, value_states, pose_depth, hint_weight, gain, band_offsets, control_flags = [
            pltpu.with_memory_space_constraint(a, pltpu.HBM)
            for a in (
                queries, key_states, value_states, pose_depth, hint_weight, gain, band_offsets, control_flags
            )
        ]
        cuts = [(sum(SLICES[:c]) * HEAD_DIM, n * HEAD_DIM) for c, n in enumerate(SLICES)]
        far_wire, side_wire = [], []

        def after(values, *deps):
            deps = [d for d in deps if d is not None]
            return lax.optimization_barrier((values, deps))[0] if deps else values

        def back(wire, depth):
            return wire[-depth] if 0 < depth <= len(wire) else None

        def far_group(parts, depth, gate=None):
            got = []
            for part, k in zip(parts, (3, 2)):
                part = after(part, back(far_wire, depth), gate)
                got.append(lax.ppermute(part, "tm", across[k]))
                far_wire.append(got[-1])
                gate = None
            return [got[1], got[0]]

        def near_group(parts):
            return [parts[0], lax.ppermute(parts[1], "tm", across[1])]

        def along(last, start):
            last, start = after([last, start], back(side_wire, 2))
            got = (lax.ppermute(last, "tm", upward), lax.ppermute(start, "tm", downward))
            side_wire.append(got)
            return got

        n = len(cuts)
        size = frames * queries.shape[1]
        pairs, asked, sides, mixed, edge = {}, {}, {}, {}, {}
        for c, (first, width) in enumerate(cuts):
            what = ([key_states, value_states], [pose_depth, band_offsets, control_flags] if c == 0 else [])
            far = far_group(pack(me, (3, 2), *what, quarter, first, width), 4, edge.get(c - 1))
            pairs[c] = [*near_group(pack(me, (0, 1), *what, quarter, first, width)), *far]
            edge[c] = edges(me, pairs[c])
            sides[c] = along(*edge[c])
        *near, weight, share = pack_own(me, queries, hint_weight, gain, quarter)
        near, shares = near_group(near), (weight, share)
        for c, (first, width) in enumerate(cuts):
            far = far_group(pack(me, (3, 2), [queries], [], quarter, first, width), 4, edge.get(n + c - 1))
            asked[c] = [*near, *far]
        setting = None
        for c, (first, width) in enumerate(cuts):
            got = hint_branch(me, pairs[c], asked[c], *sides[c], *shares, setting, spans, frames, first)
            setting = got[4:] if setting is None else setting
            mixed[c] = [got[3], got[0], *along(got[1], got[2])]
        parts = []
        for c, (first, width) in enumerate(cuts):
            keys = after(mixed[c][0], mixed[n - 1][1]) if True and c < n - 1 else mixed[c][0]
            got = base_block(me, asked[c], keys, *mixed[c][1:], setting[1], spans, first)
            parts.append([*near_group(got[:2]), *far_group(got[:1:-1], 2)])
        out = None
        for c, (first, width) in enumerate(cuts):
            out = place(me, parts[c], out, model_width, quarter, first)
        return out

    return jax.shard_map(
        body,
        mesh=mesh,
        in_specs=(
            P(("grp", "tm"), None, None),
            P(("grp", "tm"), None, None),
            P(("grp", "tm"), None, None),
            P(("grp", "tm"), None, None),
            P(),
            P(),
            P(("grp", "tm"), None),
            P(("grp", "tm")),
        ),
        out_specs=P(("grp", "tm"), None, None),
        check_vma=False,
    )
```

```python
import jax
import jax.numpy as jnp
from jax import lax
from jax.experimental import pallas as pl
from jax.experimental.pallas import tpu as pltpu
from jax.sharding import PartitionSpec as P

HEAD_DIM = 128
BAND = 2
GROUP = 4
SLICES = (5, 5)
META = 8
PIECE = 16
F32 = jnp.float32
BF16 = jnp.bfloat16
I32 = jnp.int32
VMEM = pl.BlockSpec(memory_space=pltpu.VMEM)
SMEM = pl.BlockSpec(memory_space=pltpu.SMEM)
HBM = pl.BlockSpec(memory_space=pltpu.HBM)


def run(kernel, name, ins, outs, scratch, copies, scalars=(), where=VMEM, to=VMEM, aliases=None, us=1.0):
    a, b, c, d = len(scalars), len(ins), len(outs), len(scratch)

    def body(*refs):
        kernel(refs[:a], refs[a : a + b], refs[a + b : a + b + c], refs[a + b + c : a + b + c + d], refs[-1])

    return pl.pallas_call(
        body,
        out_shape=list(outs),
        in_specs=[SMEM] * a + (where if isinstance(where, list) else [where] * b),
        out_specs=[to] * c,
        scratch_shapes=[*scratch, pltpu.SemaphoreType.DMA((max(copies, 1),))],
        input_output_aliases=aliases or {},
        compiler_params=pltpu.CompilerParams(vmem_limit_bytes=16 * 1024 * 1024),
        cost_estimate=pl.CostEstimate(flops=1, bytes_accessed=int(us * 3.4e6), transcendentals=0),
        name=name,
    )(*scalars, *ins)


def move(pairs, sems):
    copies = [pltpu.make_async_copy(s, d, sems.at[i]) for i, (s, d) in enumerate(pairs)]
    for copy in copies:
        copy.start()
    for copy in copies:
        copy.wait()


def lanes(me, quarter, first, width):
    return pl.ds(pl.multiple_of(me * quarter + first, HEAD_DIM), width)


def rows(shape, dtype=BF16):
    return jax.ShapeDtypeStruct(shape, dtype)


def notes_at(i, width):
    blocks = width // HEAD_DIM
    return PIECE * (i // blocks), HEAD_DIM * (i % blocks)


def note_rows(pieces, width):
    return PIECE * -(-pieces * HEAD_DIM // width)


def read_note(ref, top, left, width, i):
    down, right = notes_at(i, width)
    return ref[top + down : top + down + PIECE, left + right : left + right + HEAD_DIM]


def pack(me, ks, arrays, notes, quarter, first, width):
    frames, toks, _ = arrays[0].shape
    size = frames * toks
    pieces = size // PIECE + 1 if notes else 0
    base = len(arrays) * size

    def kernel(scalars, ins, outs, scratch, sems):
        mine = scalars[0][0]
        pairs = list(zip(ins[len(arrays) :], scratch))
        for i, k in enumerate(ks):
            where = lanes(mine ^ k, quarter, first, width)
            for j in range(len(arrays)):
                for f in range(frames):
                    pairs.append((ins[j].at[f, :, where], outs[i].at[pl.ds(j * size + f * toks, toks)]))
        copies = [pltpu.make_async_copy(s, d, sems.at[i]) for i, (s, d) in enumerate(pairs)]
        for copy in copies:
            copy.start()
        if notes:
            for copy in copies[: len(notes)]:
                copy.wait()
            patches, offsets, flags = scratch
            spans = offsets.shape[1]
            row = lax.broadcasted_iota(I32, (PIECE, HEAD_DIM), 0)
            col = lax.broadcasted_iota(I32, (PIECE, HEAD_DIM), 1)
            block = jnp.zeros((PIECE, HEAD_DIM), F32)
            for f in range(frames):
                for j in range(spans):
                    block = jnp.where((row == f) & (col == j), offsets[f, j].astype(F32), block)
                block = jnp.where((row == f) & (col == spans), flags[f].astype(F32), block)
            per = toks // PIECE
            for i in range(pieces):
                top, left = notes_at(i, width)
                if i == pieces - 1:
                    piece = block.astype(BF16)
                else:
                    piece = patches[i // per, PIECE * (i % per) : PIECE * (i % per + 1)]
                for out in outs:
                    out[base + top : base + top + PIECE, left : left + HEAD_DIM] = piece
        for copy in copies[len(notes) :]:
            copy.wait()

    scratch = []
    if notes:
        pose, offsets, flags = notes
        scratch = [pltpu.VMEM(pose.shape, BF16), pltpu.SMEM(offsets.shape, I32), pltpu.SMEM(flags.shape, I32)]
    outs = [rows((base + note_rows(pieces, width), width))] * len(ks)
    copies = frames * len(arrays) * len(ks) + len(notes)
    return run(kernel, "pack", [*arrays, *notes], outs, scratch, copies, [me], where=HBM)


def pack_own(me, queries, weight, gain, quarter):
    frames, toks, _ = queries.shape

    def kernel(scalars, ins, outs, scratch, sems):
        mine = scalars[0][0]
        pairs = []
        for k in range(2):
            for f in range(frames):
                where = lanes(mine ^ k, quarter, 0, quarter)
                pairs.append((ins[0].at[f, :, where], outs[k].at[pl.ds(f * toks, toks)]))
        for i in (1, 2):
            pairs.append((ins[i].at[:, lanes(mine, quarter, 0, quarter)], outs[1 + i]))
        move(pairs, sems)

    outs = [rows((frames * toks, quarter))] * 2 + [rows((weight.shape[0], quarter)), rows((1, quarter), F32)]
    return run(kernel, "pack_own", [queries, weight, gain], outs, [], 2 * frames + 2, [me], where=HBM)


def edges(me, parts):
    def kernel(scalars, ins, outs, scratch, sems):
        mine = scalars[0][0]
        for out, owner in zip(outs, (GROUP - 1, 0)):
            for k in range(GROUP):

                @pl.when((mine ^ k) == owner)
                def _(out=out, k=k):
                    out[...] = ins[k][...]

    shape = rows(parts[0].shape)
    return run(kernel, "edges", parts, [shape, shape], [], 0, [me], us=0.2)


def attend(jobs):
    scores = [
        lax.dot_general(query, keys, (((1,), (1,)), ((), ())), preferred_element_type=F32) * HEAD_DIM ** (-0.5)
        for query, keys, _ in jobs
    ]
    tops = [jnp.max(x, axis=1, keepdims=True) for x in scores]
    scores = [jnp.exp(x - top) for x, top in zip(scores, tops)]
    scales = [1.0 / jnp.sum(x, axis=1, keepdims=True) for x in scores]
    weights = [(x * scale).astype(BF16) for x, scale in zip(scores, scales)]
    return [
        jnp.dot(w, values, preferred_element_type=F32).astype(BF16) for w, (_, _, values) in zip(weights, jobs)
    ]


def band(ref, spots, cols):
    return jnp.concatenate([ref[s, :, cols] for s in spots], axis=0)


def hint_branch(me, pairs, queries, before, after, weight, gain, setting, spans, frames, first):
    size, width = queries[-1].shape
    toks = size // frames
    lead = setting is None
    total, wide = GROUP * frames, GROUP * frames + 2 * BAND
    heads = [slice(h * HEAD_DIM, (h + 1) * HEAD_DIM) for h in range(width // HEAD_DIM)]
    own_lanes = slice(first, first + width)

    def kernel(scalars, ins, outs, scratch, sems):
        mine = scalars[0][0]
        sources, qs = [*ins[:GROUP], *ins[2 * GROUP : 2 * GROUP + 2]], ins[GROUP : 2 * GROUP]
        w_ref, g_ref = ins[2 * GROUP + 2 : 2 * GROUP + 4]
        mixed, up, down, keys_out = outs[:4]
        q_s, k_s, c_s = scratch[:3]
        pieces, per = size // PIECE, toks // PIECE

        def taken(k, j, f):
            if j < 2:
                return sources[k][j * size + f * toks : j * size + (f + 1) * toks]
            return qs[k][f * toks : (f + 1) * toks, own_lanes if k < 2 else slice(None)]

        def note(k, i):
            return read_note(sources[k], 2 * size, 0, width, i)

        if lead:
            pose_out, meta_out = outs[4:]
            meta = scratch[3]
            for k in range(GROUP):
                meta_out[mine ^ k] = note(k, pieces).astype(F32).astype(I32)[:META]
            known = pltpu.make_async_copy(meta_out, meta, sems.at[0])
            known.start()
        else:
            meta = scalars[1]
        for k in range(GROUP + 2):
            at = BAND + (mine ^ k) * frames if k < GROUP else (0 if k == GROUP else BAND + total)
            if lead:
                patches = [jnp.concatenate([note(k, f * per + i) for i in range(per)], axis=0) for f in range(frames)]
                for f in range(frames):
                    pose_out[at + f] = patches[f]
            else:
                patches = [ins[-1][at + f] for f in range(frames)]
            hint = jnp.dot(jnp.concatenate(patches, axis=0), w_ref[:, own_lanes], preferred_element_type=F32)
            hint = hint.astype(BF16).astype(F32)
            for f in range(frames):
                own = hint[f * toks : (f + 1) * toks]
                key = taken(k, 0, f)
                keys_out[at + f] = key
                k_s[at + f] = (key.astype(F32) + own).astype(BF16)
                c_s[at + f] = (taken(k, 1, f).astype(F32) + own).astype(BF16)
                if k < GROUP:
                    q_s[k * frames + f] = (taken(k, 2, f).astype(F32) + own).astype(BF16)
        if lead:
            known.wait()
        at, jobs = [], []
        for k in range(GROUP):
            for r in range(frames):
                s = mine ^ k
                f = s * frames + r
                spots = [BAND + f + meta[s, r, j] for j in range(spans)]
                for cols in heads:
                    at.append((k, r, f, meta[s, r, spans].astype(F32), cols))
                    jobs.append((q_s[k * frames + r, :, cols], band(k_s, spots, cols), band(c_s, spots, cols)))
        for (k, r, f, flag, cols), out in zip(at, attend(jobs)):
            scale = g_ref[:, first + cols.start : first + cols.stop]
            residual = (flag * scale * out.astype(F32)).astype(BF16)
            mixed[f, :, cols] = (taken(k, 1, r)[:, cols].astype(F32) + residual.astype(F32)).astype(BF16)
        up[...] = mixed[total - BAND :]
        down[...] = mixed[:BAND]

    outs = [rows((total, toks, width)), rows((BAND, toks, width)), rows((BAND, toks, width)), rows((wide, toks, width))]
    scratch = [
        pltpu.VMEM((total, toks, width), BF16),
        pltpu.VMEM((wide, toks, width), BF16),
        pltpu.VMEM((wide, toks, width), BF16),
    ]
    ins = [*pairs, *queries, before, after, weight, gain]
    scalars = [me]
    if lead:
        outs += [rows((wide, toks, HEAD_DIM)), rows((GROUP, META, HEAD_DIM), I32)]
        scratch.append(pltpu.SMEM((GROUP, META, HEAD_DIM), I32))
    else:
        ins.append(setting[0])
        scalars.append(setting[1])
    return run(kernel, "hint_branch", ins, outs, scratch, 1, scalars, us=0.5 + 0.8 * len(heads))


def base_block(me, queries, keys, mixed, mixed_before, mixed_after, meta, spans, first):
    total, toks, width = mixed.shape
    frames, wide = total // GROUP, total + 2 * BAND
    heads = [slice(h * HEAD_DIM, (h + 1) * HEAD_DIM) for h in range(width // HEAD_DIM)]

    def kernel(scalars, ins, outs, scratch, sems):
        mine, meta = scalars[0][0], scalars[1]
        k_ref, m_s = ins[GROUP], scratch[0]
        m_s[BAND : BAND + total] = ins[GROUP + 1][...]
        m_s[:BAND] = ins[GROUP + 2][...]
        m_s[BAND + total :] = ins[GROUP + 3][...]
        at, jobs = [], []
        for k in range(GROUP):
            for r in range(frames):
                s = mine ^ k
                spots = [BAND + s * frames + r + meta[s, r, j] for j in range(spans)]
                for cols in heads:
                    at.append((k, r, cols))
                    left = first if k < 2 else 0
                    query = ins[k][r * toks : (r + 1) * toks, left + cols.start : left + cols.stop]
                    jobs.append((query, band(k_ref, spots, cols), band(m_s, spots, cols)))
        for (k, r, cols), out in zip(at, attend(jobs)):
            outs[k][r, :, cols] = out

    ins = [*queries, keys, mixed, mixed_before, mixed_after]
    scratch = [pltpu.VMEM((wide, toks, width), BF16)]
    outs = [rows((frames, toks, width))] * GROUP
    return run(kernel, "base_block", ins, outs, scratch, 0, [me, meta], us=0.7 * len(heads))


def place(me, parts, into, model_width, quarter, first):
    frames, toks, width = parts[0].shape

    def kernel(scalars, ins, outs, scratch, sems):
        mine = scalars[0][0]
        move([(ins[k], outs[0].at[:, :, lanes(mine ^ k, quarter, first, width)]) for k in range(GROUP)], sems)

    held = [] if into is None else [into]
    return run(
        kernel,
        "place",
        [*parts, *held],
        [rows((frames, toks, model_width))],
        [],
        GROUP,
        [me],
        where=[VMEM] * GROUP + [HBM] * len(held),
        to=HBM,
        aliases={} if into is None else {1 + GROUP: 0},
        us=0.8,
    )[0]


def solution(mesh):
    count = mesh.shape["tm"]
    assert count % GROUP == 0
    across = [[(i, i ^ k) for i in range(count)] for k in range(GROUP)]
    upward = [(i, (i + GROUP) % count) for i in range(count)]
    downward = [(i, (i - GROUP) % count) for i in range(count)]

    def exchange(parts):
        return [parts[0]] + [lax.ppermute(parts[k], "tm", across[k]) for k in range(1, GROUP)]

    def body(queries, key_states, value_states, pose_depth, hint_weight, control_gain, band_offsets, control_flags):
        frames, _, model_width = queries.shape
        spans = band_offsets.shape[1]
        quarter = model_width // GROUP
        assert frames == BAND and sum(SLICES) * HEAD_DIM == quarter
        me = lax.rem(lax.axis_index("tm"), GROUP).astype(I32).reshape(1)
        gain = control_gain.reshape(1, -1)
        queries, key_states, value_states, pose_depth, hint_weight, gain, band_offsets, control_flags = [
            pltpu.with_memory_space_constraint(a, pltpu.HBM)
            for a in (
                queries, key_states, value_states, pose_depth, hint_weight, gain, band_offsets, control_flags
            )
        ]
        cuts = [(sum(SLICES[:c]) * HEAD_DIM, n * HEAD_DIM) for c, n in enumerate(SLICES)]
        far_wire, side_wire = [], []

        def after(values, *deps):
            deps = [d for d in deps if d is not None]
            return lax.optimization_barrier((values, deps))[0] if deps else values

        def back(wire, depth):
            return wire[-depth] if 0 < depth <= len(wire) else None

        def far_group(parts, depth, gate=None):
            got = []
            for part, k in zip(parts, (3, 2)):
                part = after(part, back(far_wire, depth), gate)
                got.append(lax.ppermute(part, "tm", across[k]))
                far_wire.append(got[-1])
                gate = None
            return [got[1], got[0]]

        def near_group(parts):
            return [parts[0], lax.ppermute(parts[1], "tm", across[1])]

        def along(last, start):
            last, start = after([last, start], back(side_wire, 2))
            got = (lax.ppermute(last, "tm", upward), lax.ppermute(start, "tm", downward))
            side_wire.append(got)
            return got

        n = len(cuts)
        size = frames * queries.shape[1]
        pairs, asked, sides, mixed, edge = {}, {}, {}, {}, {}
        for c, (first, width) in enumerate(cuts):
            what = ([key_states, value_states], [pose_depth, band_offsets, control_flags] if c == 0 else [])
            far = far_group(pack(me, (3, 2), *what, quarter, first, width), 3, edge.get(c - 2))
            pairs[c] = [*near_group(pack(me, (0, 1), *what, quarter, first, width)), *far]
            edge[c] = edges(me, pairs[c])
            sides[c] = along(*edge[c])
        *near, weight, share = pack_own(me, queries, hint_weight, gain, quarter)
        near, shares = near_group(near), (weight, share)
        for c, (first, width) in enumerate(cuts):
            far = far_group(pack(me, (3, 2), [queries], [], quarter, first, width), 3, sides[0] if c == n - 1 else edge.get(n + c - 2))
            asked[c] = [*near, *far]
        setting = None
        for c, (first, width) in enumerate(cuts):
            got = hint_branch(me, pairs[c], asked[c], *sides[c], *shares, setting, spans, frames, first)
            setting = got[4:] if setting is None else setting
            mixed[c] = [got[3], got[0], *along(got[1], got[2])]
        parts = []
        for c, (first, width) in enumerate(cuts):
            keys = after(mixed[c][0], mixed[n - 1][1]) if True and c < n - 1 else mixed[c][0]
            got = base_block(me, asked[c], keys, *mixed[c][1:], setting[1], spans, first)
            parts.append([*near_group(got[:2]), *far_group(got[:1:-1], 2)])
        out = None
        for c, (first, width) in enumerate(cuts):
            out = place(me, parts[c], out, model_width, quarter, first)
        return out

    return jax.shard_map(
        body,
        mesh=mesh,
        in_specs=(
            P(("grp", "tm"), None, None),
            P(("grp", "tm"), None, None),
            P(("grp", "tm"), None, None),
            P(("grp", "tm"), None, None),
            P(),
            P(),
            P(("grp", "tm"), None),
            P(("grp", "tm")),
        ),
        out_specs=P(("grp", "tm"), None, None),
        check_vma=False,
    )
```

```python
import jax
import jax.numpy as jnp
from jax import lax
from jax.experimental import pallas as pl
from jax.experimental.pallas import tpu as pltpu
from jax.sharding import PartitionSpec as P

HEAD_DIM = 128
BAND = 2
GROUP = 4
SLICES = (5, 5)
META = 8
PIECE = 16
F32 = jnp.float32
BF16 = jnp.bfloat16
I32 = jnp.int32
VMEM = pl.BlockSpec(memory_space=pltpu.VMEM)
SMEM = pl.BlockSpec(memory_space=pltpu.SMEM)
HBM = pl.BlockSpec(memory_space=pltpu.HBM)


def run(kernel, name, ins, outs, scratch, copies, scalars=(), where=VMEM, to=VMEM, aliases=None, us=1.0):
    a, b, c, d = len(scalars), len(ins), len(outs), len(scratch)

    def body(*refs):
        kernel(refs[:a], refs[a : a + b], refs[a + b : a + b + c], refs[a + b + c : a + b + c + d], refs[-1])

    return pl.pallas_call(
        body,
        out_shape=list(outs),
        in_specs=[SMEM] * a + (where if isinstance(where, list) else [where] * b),
        out_specs=[to] * c,
        scratch_shapes=[*scratch, pltpu.SemaphoreType.DMA((max(copies, 1),))],
        input_output_aliases=aliases or {},
        compiler_params=pltpu.CompilerParams(vmem_limit_bytes=16 * 1024 * 1024),
        cost_estimate=pl.CostEstimate(flops=1, bytes_accessed=int(us * 3.4e6), transcendentals=0),
        name=name,
    )(*scalars, *ins)


def move(pairs, sems):
    copies = [pltpu.make_async_copy(s, d, sems.at[i]) for i, (s, d) in enumerate(pairs)]
    for copy in copies:
        copy.start()
    for copy in copies:
        copy.wait()


def lanes(me, quarter, first, width):
    return pl.ds(pl.multiple_of(me * quarter + first, HEAD_DIM), width)


def rows(shape, dtype=BF16):
    return jax.ShapeDtypeStruct(shape, dtype)


def notes_at(i, width):
    blocks = width // HEAD_DIM
    return PIECE * (i // blocks), HEAD_DIM * (i % blocks)


def note_rows(pieces, width):
    return PIECE * -(-pieces * HEAD_DIM // width)


def read_note(ref, top, left, width, i):
    down, right = notes_at(i, width)
    return ref[top + down : top + down + PIECE, left + right : left + right + HEAD_DIM]


def pack(me, ks, arrays, notes, quarter, first, width):
    frames, toks, _ = arrays[0].shape
    size = frames * toks
    pieces = size // PIECE + 1 if notes else 0
    base = len(arrays) * size

    def kernel(scalars, ins, outs, scratch, sems):
        mine = scalars[0][0]
        pairs = list(zip(ins[len(arrays) :], scratch))
        for i, k in enumerate(ks):
            where = lanes(mine ^ k, quarter, first, width)
            for j in range(len(arrays)):
                for f in range(frames):
                    pairs.append((ins[j].at[f, :, where], outs[i].at[pl.ds(j * size + f * toks, toks)]))
        copies = [pltpu.make_async_copy(s, d, sems.at[i]) for i, (s, d) in enumerate(pairs)]
        for copy in copies:
            copy.start()
        if notes:
            for copy in copies[: len(notes)]:
                copy.wait()
            patches, offsets, flags = scratch
            spans = offsets.shape[1]
            row = lax.broadcasted_iota(I32, (PIECE, HEAD_DIM), 0)
            col = lax.broadcasted_iota(I32, (PIECE, HEAD_DIM), 1)
            block = jnp.zeros((PIECE, HEAD_DIM), F32)
            for f in range(frames):
                for j in range(spans):
                    block = jnp.where((row == f) & (col == j), offsets[f, j].astype(F32), block)
                block = jnp.where((row == f) & (col == spans), flags[f].astype(F32), block)
            per = toks // PIECE
            for i in range(pieces):
                top, left = notes_at(i, width)
                if i == pieces - 1:
                    piece = block.astype(BF16)
                else:
                    piece = patches[i // per, PIECE * (i % per) : PIECE * (i % per + 1)]
                for out in outs:
                    out[base + top : base + top + PIECE, left : left + HEAD_DIM] = piece
        for copy in copies[len(notes) :]:
            copy.wait()

    scratch = []
    if notes:
        pose, offsets, flags = notes
        scratch = [pltpu.VMEM(pose.shape, BF16), pltpu.SMEM(offsets.shape, I32), pltpu.SMEM(flags.shape, I32)]
    outs = [rows((base + note_rows(pieces, width), width))] * len(ks)
    copies = frames * len(arrays) * len(ks) + len(notes)
    return run(kernel, "pack", [*arrays, *notes], outs, scratch, copies, [me], where=HBM)


def pack_own(me, queries, weight, gain, quarter):
    frames, toks, _ = queries.shape

    def kernel(scalars, ins, outs, scratch, sems):
        mine = scalars[0][0]
        pairs = []
        for k in range(2):
            for f in range(frames):
                where = lanes(mine ^ k, quarter, 0, quarter)
                pairs.append((ins[0].at[f, :, where], outs[k].at[pl.ds(f * toks, toks)]))
        for i in (1, 2):
            pairs.append((ins[i].at[:, lanes(mine, quarter, 0, quarter)], outs[1 + i]))
        move(pairs, sems)

    outs = [rows((frames * toks, quarter))] * 2 + [rows((weight.shape[0], quarter)), rows((1, quarter), F32)]
    return run(kernel, "pack_own", [queries, weight, gain], outs, [], 2 * frames + 2, [me], where=HBM)


def edges(me, parts):
    def kernel(scalars, ins, outs, scratch, sems):
        mine = scalars[0][0]
        for out, owner in zip(outs, (GROUP - 1, 0)):
            for k in range(GROUP):

                @pl.when((mine ^ k) == owner)
                def _(out=out, k=k):
                    out[...] = ins[k][...]

    shape = rows(parts[0].shape)
    return run(kernel, "edges", parts, [shape, shape], [], 0, [me], us=0.2)


def attend(jobs):
    scores = [
        lax.dot_general(query, keys, (((1,), (1,)), ((), ())), preferred_element_type=F32) * HEAD_DIM ** (-0.5)
        for query, keys, _ in jobs
    ]
    tops = [jnp.max(x, axis=1, keepdims=True) for x in scores]
    scores = [jnp.exp(x - top) for x, top in zip(scores, tops)]
    scales = [1.0 / jnp.sum(x, axis=1, keepdims=True) for x in scores]
    weights = [(x * scale).astype(BF16) for x, scale in zip(scores, scales)]
    return [
        jnp.dot(w, values, preferred_element_type=F32).astype(BF16) for w, (_, _, values) in zip(weights, jobs)
    ]


def band(ref, spots, cols):
    return jnp.concatenate([ref[s, :, cols] for s in spots], axis=0)


def hint_branch(me, pairs, queries, before, after, weight, gain, setting, spans, frames, first):
    size, width = queries[-1].shape
    toks = size // frames
    lead = setting is None
    total, wide = GROUP * frames, GROUP * frames + 2 * BAND
    heads = [slice(h * HEAD_DIM, (h + 1) * HEAD_DIM) for h in range(width // HEAD_DIM)]
    own_lanes = slice(first, first + width)

    def kernel(scalars, ins, outs, scratch, sems):
        mine = scalars[0][0]
        sources, qs = [*ins[:GROUP], *ins[2 * GROUP : 2 * GROUP + 2]], ins[GROUP : 2 * GROUP]
        w_ref, g_ref = ins[2 * GROUP + 2 : 2 * GROUP + 4]
        mixed, up, down, keys_out = outs[:4]
        q_s, k_s, c_s = scratch[:3]
        pieces, per = size // PIECE, toks // PIECE

        def taken(k, j, f):
            if j < 2:
                return sources[k][j * size + f * toks : j * size + (f + 1) * toks]
            return qs[k][f * toks : (f + 1) * toks, own_lanes if k < 2 else slice(None)]

        def note(k, i):
            return read_note(sources[k], 2 * size, 0, width, i)

        if lead:
            pose_out, meta_out = outs[4:]
            meta = scratch[3]
            for k in range(GROUP):
                meta_out[mine ^ k] = note(k, pieces).astype(F32).astype(I32)[:META]
            known = pltpu.make_async_copy(meta_out, meta, sems.at[0])
            known.start()
        else:
            meta = scalars[1]
        for k in range(GROUP + 2):
            at = BAND + (mine ^ k) * frames if k < GROUP else (0 if k == GROUP else BAND + total)
            if lead:
                patches = [jnp.concatenate([note(k, f * per + i) for i in range(per)], axis=0) for f in range(frames)]
                for f in range(frames):
                    pose_out[at + f] = patches[f]
            else:
                patches = [ins[-1][at + f] for f in range(frames)]
            hint = jnp.dot(jnp.concatenate(patches, axis=0), w_ref[:, own_lanes], preferred_element_type=F32)
            hint = hint.astype(BF16).astype(F32)
            for f in range(frames):
                own = hint[f * toks : (f + 1) * toks]
                key = taken(k, 0, f)
                keys_out[at + f] = key
                k_s[at + f] = (key.astype(F32) + own).astype(BF16)
                c_s[at + f] = (taken(k, 1, f).astype(F32) + own).astype(BF16)
                if k < GROUP:
                    q_s[k * frames + f] = (taken(k, 2, f).astype(F32) + own).astype(BF16)
        if lead:
            known.wait()
        at, jobs = [], []
        for k in range(GROUP):
            for r in range(frames):
                s = mine ^ k
                f = s * frames + r
                spots = [BAND + f + meta[s, r, j] for j in range(spans)]
                for cols in heads:
                    at.append((k, r, f, meta[s, r, spans].astype(F32), cols))
                    jobs.append((q_s[k * frames + r, :, cols], band(k_s, spots, cols), band(c_s, spots, cols)))
        for (k, r, f, flag, cols), out in zip(at, attend(jobs)):
            scale = g_ref[:, first + cols.start : first + cols.stop]
            residual = (flag * scale * out.astype(F32)).astype(BF16)
            mixed[f, :, cols] = (taken(k, 1, r)[:, cols].astype(F32) + residual.astype(F32)).astype(BF16)
        up[...] = mixed[total - BAND :]
        down[...] = mixed[:BAND]

    outs = [rows((total, toks, width)), rows((BAND, toks, width)), rows((BAND, toks, width)), rows((wide, toks, width))]
    scratch = [
        pltpu.VMEM((total, toks, width), BF16),
        pltpu.VMEM((wide, toks, width), BF16),
        pltpu.VMEM((wide, toks, width), BF16),
    ]
    ins = [*pairs, *queries, before, after, weight, gain]
    scalars = [me]
    if lead:
        outs += [rows((wide, toks, HEAD_DIM)), rows((GROUP, META, HEAD_DIM), I32)]
        scratch.append(pltpu.SMEM((GROUP, META, HEAD_DIM), I32))
    else:
        ins.append(setting[0])
        scalars.append(setting[1])
    return run(kernel, "hint_branch", ins, outs, scratch, 1, scalars, us=0.5 + 0.8 * len(heads))


def base_block(me, ks, queries, keys, mixed, mixed_before, mixed_after, meta, spans, first):
    total, toks, width = mixed.shape
    frames, wide = total // GROUP, total + 2 * BAND
    heads = [slice(h * HEAD_DIM, (h + 1) * HEAD_DIM) for h in range(width // HEAD_DIM)]

    def kernel(scalars, ins, outs, scratch, sems):
        mine, meta = scalars[0][0], scalars[1]
        k_ref, m_s = ins[len(ks)], scratch[0]
        m_s[BAND : BAND + total] = ins[len(ks) + 1][...]
        m_s[:BAND] = ins[len(ks) + 2][...]
        m_s[BAND + total :] = ins[len(ks) + 3][...]
        at, jobs = [], []
        for i, k in enumerate(ks):
            for r in range(frames):
                s = mine ^ k
                spots = [BAND + s * frames + r + meta[s, r, j] for j in range(spans)]
                for cols in heads:
                    at.append((i, r, cols))
                    left = first if k < 2 else 0
                    query = ins[i][r * toks : (r + 1) * toks, left + cols.start : left + cols.stop]
                    jobs.append((query, band(k_ref, spots, cols), band(m_s, spots, cols)))
        for (i, r, cols), out in zip(at, attend(jobs)):
            outs[i][r, :, cols] = out

    ins = [*queries, keys, mixed, mixed_before, mixed_after]
    scratch = [pltpu.VMEM((wide, toks, width), BF16)]
    outs = [rows((frames, toks, width))] * len(ks)
    return run(kernel, "base_block", ins, outs, scratch, 0, [me, meta], us=0.7 * len(heads))


def place(me, parts, into, model_width, quarter, first):
    frames, toks, width = parts[0].shape

    def kernel(scalars, ins, outs, scratch, sems):
        mine = scalars[0][0]
        move([(ins[k], outs[0].at[:, :, lanes(mine ^ k, quarter, first, width)]) for k in range(GROUP)], sems)

    held = [] if into is None else [into]
    return run(
        kernel,
        "place",
        [*parts, *held],
        [rows((frames, toks, model_width))],
        [],
        GROUP,
        [me],
        where=[VMEM] * GROUP + [HBM] * len(held),
        to=HBM,
        aliases={} if into is None else {1 + GROUP: 0},
        us=0.8,
    )[0]


def solution(mesh):
    count = mesh.shape["tm"]
    assert count % GROUP == 0
    across = [[(i, i ^ k) for i in range(count)] for k in range(GROUP)]
    upward = [(i, (i + GROUP) % count) for i in range(count)]
    downward = [(i, (i - GROUP) % count) for i in range(count)]

    def exchange(parts):
        return [parts[0]] + [lax.ppermute(parts[k], "tm", across[k]) for k in range(1, GROUP)]

    def body(queries, key_states, value_states, pose_depth, hint_weight, control_gain, band_offsets, control_flags):
        frames, _, model_width = queries.shape
        spans = band_offsets.shape[1]
        quarter = model_width // GROUP
        assert frames == BAND and sum(SLICES) * HEAD_DIM == quarter
        me = lax.rem(lax.axis_index("tm"), GROUP).astype(I32).reshape(1)
        gain = control_gain.reshape(1, -1)
        queries, key_states, value_states, pose_depth, hint_weight, gain, band_offsets, control_flags = [
            pltpu.with_memory_space_constraint(a, pltpu.HBM)
            for a in (
                queries, key_states, value_states, pose_depth, hint_weight, gain, band_offsets, control_flags
            )
        ]
        cuts = [(sum(SLICES[:c]) * HEAD_DIM, n * HEAD_DIM) for c, n in enumerate(SLICES)]
        far_wire, side_wire = [], []

        def after(values, *deps):
            deps = [d for d in deps if d is not None]
            return lax.optimization_barrier((values, deps))[0] if deps else values

        def back(wire, depth):
            return wire[-depth] if 0 < depth <= len(wire) else None

        def far_group(parts, depth, gate=None):
            got = []
            for part, k in zip(parts, (3, 2)):
                part = after(part, back(far_wire, depth), gate)
                got.append(lax.ppermute(part, "tm", across[k]))
                far_wire.append(got[-1])
                gate = None
            return [got[1], got[0]]

        def near_group(parts):
            return [parts[0], lax.ppermute(parts[1], "tm", across[1])]

        def along(last, start):
            last, start = after([last, start], back(side_wire, 2))
            got = (lax.ppermute(last, "tm", upward), lax.ppermute(start, "tm", downward))
            side_wire.append(got)
            return got

        n = len(cuts)
        size = frames * queries.shape[1]
        pairs, asked, sides, mixed, edge = {}, {}, {}, {}, {}
        for c, (first, width) in enumerate(cuts):
            what = ([key_states, value_states], [pose_depth, band_offsets, control_flags] if c == 0 else [])
            far = far_group(pack(me, (3, 2), *what, quarter, first, width), 3, edge.get(c - 2))
            pairs[c] = [*near_group(pack(me, (0, 1), *what, quarter, first, width)), *far]
            edge[c] = edges(me, pairs[c])
            sides[c] = along(*edge[c])
        *near, weight, share = pack_own(me, queries, hint_weight, gain, quarter)
        near, shares = near_group(near), (weight, share)
        for c, (first, width) in enumerate(cuts):
            far = far_group(pack(me, (3, 2), [queries], [], quarter, first, width), 3, sides[0] if c == n - 1 else edge.get(n + c - 2))
            asked[c] = [*near, *far]
        setting = None
        for c, (first, width) in enumerate(cuts):
            got = hint_branch(me, pairs[c], asked[c], *sides[c], *shares, setting, spans, frames, first)
            setting = got[4:] if setting is None else setting
            mixed[c] = [got[3], got[0], *along(got[1], got[2])]
        parts = []
        for c, (first, width) in enumerate(cuts):
            keys = after(mixed[c][0], mixed[n - 1][1]) if True and c < n - 1 else mixed[c][0]
            rest = (keys, *mixed[c][1:], setting[1], spans, first)
            sent = base_block(me, (3, 2), asked[c][:1:-1], *rest)
            far = far_group(sent, 2)
            got = base_block(after(me, sent[0]), (0, 1), asked[c][:2], *rest)
            parts.append([*near_group(got), *far])
        out = None
        for c, (first, width) in enumerate(cuts):
            out = place(me, parts[c], out, model_width, quarter, first)
        return out

    return jax.shard_map(
        body,
        mesh=mesh,
        in_specs=(
            P(("grp", "tm"), None, None),
            P(("grp", "tm"), None, None),
            P(("grp", "tm"), None, None),
            P(("grp", "tm"), None, None),
            P(),
            P(),
            P(("grp", "tm"), None),
            P(("grp", "tm")),
        ),
        out_specs=P(("grp", "tm"), None, None),
        check_vma=False,
    )
```
